32 devices in a mesh: gx: 4 (over y, core), gy: 2 (over x), gz: 4 (over z).
Axes of the slice: x: 2, y: 2, z: 4, core: 2. Of those that a mesh axis runs over, the one named last changes fastest.
Arguments:
- initial_hydraulic_head: float32 [1024, 128], P(('gx', 'gy', 'gz')), may hold values from -6 to 6
- well_discharge: float32 [1024, 128], P(('gx', 'gy', 'gz')), may hold values from -6 to 6
- local_facet_coupling: bfloat16 [1024, 128, 128], P(('gx', 'gy', 'gz')), may hold values from -0.25 to 0.25
- diagonal_capacity: float32 [1024, 128], P(('gx', 'gy', 'gz')), may hold values from 0.5 to 2
- crossing_permeability: float32 [1024, 4], P(('gx', 'gy', 'gz')), may hold values from 0.3 to 3
- crossing_partner_number: int32 [1024, 4], P(('gx', 'gy', 'gz')), may hold values from 0 to 255, as said below
- liquid_thermal_state: float32 [1024, 128], P(('gx', 'gy', 'gz')), may hold values from -6 to 6
- transfer_factor: float32 [1024, 128], P(('gx', 'gy', 'gz')), may hold values from 0.1 to 1
- host_voxel_number: int32 [1024, 128], P(('gx', 'gy', 'gz')), may hold values from 0 to 65535
- stone_thermal_state: float32 [64, 64, 512], P('gx', 'gy', 'gz'), may hold values from -6 to 6
- matrix_diffusivity: float32 [64, 64, 512], P('gx', 'gy', 'gz'), may hold values from 0.02 to 0.16
Outputs:
- updated_hydraulic_head: float32 [1024, 128], P(('gx', 'gy', 'gz'))
- diffused_thermal_state: float32 [64, 64, 512], P('gx', 'gy', 'gz')
The draws below stay inside these ranges and needn't reach their ends.
Inputs may be any that keep to these rules, and one draw needn't show every extreme that they name: `crossing_partner_number`: coupling ids name blocks of devices with the same gz index: c // 32 is the index on gx+gy of the owning device and c % 32 the block on it. The 128 couplings of one device name the blocks of any one device of its group at most 32 times, and exactly 32 times for some device.
All inputs are finite; a program needn't handle non-finite values.
Results may differ from the reference program's by a relative error of at most 0.00053.
Values sent between devices are 32-bit elements; how exact they have to be, the bound alone decides.
No kernel may reach another device: no remote copies, remote signals or barrier semaphores. Data moves between devices by JAX's collectives and lax.ppermute only.
A program may use at most 64 MiB of HBM per device.

```python
import math
import jax
import jax.numpy as jnp
from jax import lax

TRI = 128
K = 4
SWEEPS = 3
CONDUCT = 2
NB_DEV = 32
CX = 16
CY = 32
CZ = 128
CAP = 32
FRACTURE_BLOCKS = 1024
WIDTH_X_COUNT = 64
WIDTH_Y_COUNT = 64
WIDTH_Z_COUNT = 512
N_GX = 4
N_GY = 2
N_GZ = 4
DEVICES = 32


def draw_crossing_partner_number(key, part):
    group = N_GX * N_GY
    conns = NB_DEV * K

    def one_device(device_key):
        key_first, key_pool, key_order, key_rows = jax.random.split(device_key, 4)
        first = jax.random.randint(key_first, (), 0, group)
        pool = jnp.arange((group - 1) * CAP, dtype=jnp.int32) // CAP
        others = pool + (pool >= first).astype(jnp.int32)
        chosen = others[jax.random.permutation(key_pool, (group - 1) * CAP)[:conns - CAP]]
        owners = jnp.concatenate([jnp.full((CAP,), first, jnp.int32), chosen])
        owners = owners[jax.random.permutation(key_order, conns)]
        rows = jax.random.randint(key_rows, (conns,), 0, NB_DEV)
        return (owners * NB_DEV + rows).astype(jnp.int32).reshape(NB_DEV, K)
    device_keys = jax.vmap(lambda index: jax.random.fold_in(key, index))(jnp.arange(DEVICES))
    return jax.vmap(one_device)(device_keys).reshape(NB_DEV * DEVICES, K)


def touch_ends(values, own_key, smallest, high):
    dims = values.shape
    index_at = [jax.random.randint(jax.random.fold_in(own_key, axis), (), 0, dims[axis]) for axis in range(len(dims))]
    values = values.at[tuple(index_at)].set(smallest)
    longest = dims.index(max(dims))
    index_at[longest] = (index_at[longest] + 1) % dims[longest]
    return values.at[tuple(index_at)].set(high)


def level_of(own_key, dims, pieces, low, top_value):
    factor_of, own = 1.0, jax.random.fold_in(own_key, 6)
    for dim, parts in pieces:
        heights = jnp.exp(jax.random.uniform(jax.random.fold_in(own, dim), (parts,), jnp.float32, low / len(pieces), top_value / len(pieces)))
        factor_of = factor_of * jnp.repeat(heights, dims[dim] // parts).reshape([-1 if axis == dim else 1 for axis in range(len(dims))])
    return factor_of


def bell_draw(stream_key, dims, spread, limit, pieces=(), kind=jnp.bfloat16):
    array = jax.random.normal(stream_key, dims, jnp.float32) * spread
    if len(pieces) > 0:
        array = level_of(stream_key, dims, pieces, -0.22, 0.18) * array
    return jnp.clip(array, min=-limit, max=limit).astype(kind)


def setup_inputs(seed: int = 0) -> dict:
    key_of = jax.random.split(jax.random.key(seed), 12)
    initial_hydraulic_head = bell_draw(key_of[0], (FRACTURE_BLOCKS, TRI), 1.0, 6.0, ((0, 32),), jnp.float32)
    well_discharge = bell_draw(key_of[1], (FRACTURE_BLOCKS, TRI), 1.0, 6.0, ((0, 32),), jnp.float32)
    local_facet_coupling = bell_draw(key_of[2], (FRACTURE_BLOCKS, TRI, TRI), (4 * TRI) ** -0.5, 0.25, ((0, 32),))
    diagonal_capacity = jnp.clip(0.5 + 1.5 * jax.random.uniform(key_of[3], (FRACTURE_BLOCKS, TRI), jnp.float32) ** level_of(key_of[3], (FRACTURE_BLOCKS, TRI), ((0, 32),), -0.2, 0.2), 0.5, 2.0)
    crossing_permeability = jnp.clip(jnp.exp(math.log(3.0) - 2.3025851 * jax.random.uniform(key_of[4], (FRACTURE_BLOCKS, K), jnp.float32) ** level_of(key_of[4], (FRACTURE_BLOCKS, K), ((0, 32),), -0.2, 0.2)), 0.3, 3.0)
    crossing_partner_number = draw_crossing_partner_number(jax.random.fold_in(key_of[11], 71), 0)
    liquid_thermal_state = bell_draw(key_of[6], (FRACTURE_BLOCKS, TRI), 1.0, 6.0, ((0, 32),), jnp.float32)
    transfer_factor = jnp.clip(jnp.exp(math.log(1.0) - 2.3025851 * jax.random.uniform(key_of[7], (FRACTURE_BLOCKS, TRI), jnp.float32) ** level_of(key_of[7], (FRACTURE_BLOCKS, TRI), ((0, 32),), -0.2, 0.2)), 0.1, 1.0)
    host_voxel_number = touch_ends(jax.random.randint(key_of[8], (FRACTURE_BLOCKS, TRI), 0, CX * CY * CZ), jax.random.fold_in(key_of[8], 1), 0, (CX * CY * CZ) - 1).astype(jnp.int32)
    stone_thermal_state = bell_draw(key_of[9], (WIDTH_X_COUNT, WIDTH_Y_COUNT, WIDTH_Z_COUNT), 1.0, 6.0, ((0, 4), (1, 2), (2, 4)), jnp.float32)
    matrix_diffusivity = jnp.clip(jnp.exp(math.log(0.16) - 2.0794415 * jax.random.uniform(key_of[10], (WIDTH_X_COUNT, WIDTH_Y_COUNT, WIDTH_Z_COUNT), jnp.float32) ** level_of(key_of[10], (WIDTH_X_COUNT, WIDTH_Y_COUNT, WIDTH_Z_COUNT), ((0, 4), (1, 2), (2, 4)), -0.2, 0.2)), 0.02, 0.16)
    return dict(initial_hydraulic_head=initial_hydraulic_head, well_discharge=well_discharge, local_facet_coupling=local_facet_coupling, diagonal_capacity=diagonal_capacity, crossing_permeability=crossing_permeability, crossing_partner_number=crossing_partner_number, liquid_thermal_state=liquid_thermal_state, transfer_factor=transfer_factor, host_voxel_number=host_voxel_number, stone_thermal_state=stone_thermal_state, matrix_diffusivity=matrix_diffusivity)


def diffuse_thermal_energy(temp_field, cond_field, forcing_entry):
    padded_temp = jnp.pad(temp_field, 1)
    bordered_diffusivity_array = jnp.pad(cond_field, 1)
    total = jnp.zeros_like(temp_field)
    shapes = temp_field.shape
    for axis_pos in range(3):
        for offset in (0, 2):
            starts = [1, 1, 1]
            starts[axis_pos] = offset
            neighbor_temp = lax.dynamic_slice(padded_temp, starts, shapes)
            neighbor_cond = lax.dynamic_slice(bordered_diffusivity_array, starts, shapes)
            total = total + 0.5 * (cond_field + neighbor_cond) * (neighbor_temp - temp_field)
    return temp_field + total + forcing_entry

def reference(initial_hydraulic_head, well_discharge, local_facet_coupling, diagonal_capacity, crossing_permeability, crossing_partner_number, liquid_thermal_state, transfer_factor, host_voxel_number, stone_thermal_state, matrix_diffusivity):
    blocks = initial_hydraulic_head.shape[0]
    block_dev = (jnp.arange(blocks) // NB_DEV).astype(jnp.int32)
    depth = block_dev % N_GZ
    target = (crossing_partner_number // NB_DEV * N_GZ + depth[:, None]) * NB_DEV + crossing_partner_number % NB_DEV
    denom = diagonal_capacity + lax.optimization_barrier(jnp.sum(crossing_permeability, axis=1))[:, None]
    matrix_wide = local_facet_coupling.astype(jnp.float32)
    updated_hydraulic_head = initial_hydraulic_head
    for sweep_index in range(SWEEPS):
        rounded = updated_hydraulic_head.astype(jnp.bfloat16)
        inner = jnp.einsum('bij,bj->bi', matrix_wide, rounded.astype(jnp.float32))
        across = jnp.zeros_like(updated_hydraulic_head)
        for link in range(K):
            across = across + crossing_permeability[:, link][:, None] * updated_hydraulic_head[target[:, link]]
        updated_hydraulic_head = (well_discharge + inner + across) / denom
    pos_x = block_dev // (N_GY * N_GZ)
    pos_y = block_dev // N_GZ % N_GY
    pos_z = block_dev % N_GZ
    cell_x = host_voxel_number // (CY * CZ) + (pos_x * CX)[:, None]
    cell_y = host_voxel_number // CZ % CY + (pos_y * CY)[:, None]
    cell_z = host_voxel_number % CZ + (pos_z * CZ)[:, None]
    global_cell = ((cell_x * WIDTH_Y_COUNT + cell_y) * WIDTH_Z_COUNT + cell_z).astype(jnp.int32)
    stone_linear_vector = stone_thermal_state.reshape(-1)
    flux = transfer_factor * jnp.sqrt(1.0 + updated_hydraulic_head * updated_hydraulic_head) * (liquid_thermal_state - stone_linear_vector[global_cell])
    forcing_entry = jnp.zeros(WIDTH_X_COUNT * WIDTH_Y_COUNT * WIDTH_Z_COUNT, jnp.float32).at[global_cell.reshape(-1)].add(flux.reshape(-1))
    forcing_entry = forcing_entry.reshape(WIDTH_X_COUNT, WIDTH_Y_COUNT, WIDTH_Z_COUNT)
    diffused_thermal_state = stone_thermal_state
    for sweep_index in range(CONDUCT):
        diffused_thermal_state = diffuse_thermal_energy(diffused_thermal_state, matrix_diffusivity, forcing_entry)
    return (updated_hydraulic_head, diffused_thermal_state)
```

```python
import jax
import jax.numpy as jnp
from jax import lax
from jax.experimental import pallas as pl
from jax.experimental.pallas import tpu as pltpu
from jax.sharding import PartitionSpec as P

SWEEPS = 3
CONDUCT = 2
AXES = ("gx", "gy", "gz")
GROUP = ("gx", "gy")
F32 = jnp.float32
BF16 = jnp.bfloat16
HIGH = lax.Precision.HIGHEST


def call(body, out_shape, *args, scratch=(), name=None):
    return pl.pallas_call(
        body,
        out_shape=out_shape,
        scratch_shapes=scratch,
        name=name,
        compiler_params=pltpu.CompilerParams(vmem_limit_bytes=48 << 20),
    )(*args)


def sds(shape, dtype=F32):
    return jax.ShapeDtypeStruct(shape, dtype)


def iota(shape, dim):
    return lax.broadcasted_iota(jnp.int32, shape, dim)


def dot(a, b, ca, cb, precision=None):
    return lax.dot_general(
        a, b, (((ca,), (cb,)), ((), ())), precision=precision, preferred_element_type=F32
    )


def group_size():
    return lax.axis_size("gx") * lax.axis_size("gy")


def by_pairs():
    n = group_size()
    return n <= 8 and n & (n - 1) == 0 and lax.axis_size("gx") % 2 == 0


def swap(x, k):
    n = group_size()
    return lax.ppermute(x, GROUP, [(i, i ^ k) for i in range(n)])


def meet(x):
    if not by_pairs():
        return [lax.all_gather(x, GROUP, axis=0, tiled=True)]
    n = group_size()
    low = lax.axis_size("gy")
    slots = [None] * n
    slots[0] = x
    for k in range(1, n):
        if not k & low:
            slots[k] = swap(x, k)
    for k in range(n):
        if not k & low:
            slots[k | low] = swap(slots[k], low)
    return slots


def pair_lists(count):
    first = [(i, i ^ 1 if (i ^ 1) < count else i) for i in range(count)]
    second = []
    for i in range(count):
        j = i + 1 if i % 2 else i - 1
        second.append((i, j if 0 <= j < count else i))
    return first, second


def rounds_of(axis):
    count = lax.axis_size(axis)
    return 0 if count == 1 else 1 if count == 2 else 2


def face_specs(shape, lead):
    nx, ny, nz = shape
    full = {"gx": (lead, ny, nz), "gy": (lead, nx, nz), "gz": (lead, nx * ny)}
    return [(axis, r, full[axis]) for axis in AXES for r in range(rounds_of(axis))]


def exchange(faces, specs):
    out = []
    for face, (axis, r, _) in zip(faces, specs):
        out.append(lax.ppermute(face, axis, pair_lists(lax.axis_size(axis))[r]))
    return out


def write_faces(refs, specs, fields):
    for ref, (axis, r, _) in zip(refs, specs):
        even = lax.axis_index(axis) % 2 == 0
        high = even if r == 0 else jnp.logical_not(even)
        for j, t in enumerate(fields):
            nx, ny, nz = t.shape
            if axis == "gx":
                ref[j] = jnp.where(high, t[nx - 1], t[0])
            elif axis == "gy":
                ref[j] = jnp.where(high, t[:, ny - 1, :], t[:, 0, :])
            else:
                lane = jnp.where(high, nz - 1, 0)
                pick = (iota((8, nz), 1) == lane).astype(F32)
                row = dot(pick, t.reshape(nx * ny, nz), 1, 1, HIGH)
                ref[j : j + 1, :] = row[0:1, :]


def read_ghosts(refs, specs, j):
    got = {axis: [] for axis in AXES}
    for ref, (axis, r, _) in zip(refs, specs):
        got[axis].append(ref[j : j + 1, :] if axis == "gz" else ref[j])
    ghosts = {}
    for axis in AXES:
        faces = got[axis]
        if not faces:
            ghosts[axis] = None
            continue
        index, count = lax.axis_index(axis), lax.axis_size(axis)
        even = index % 2 == 0
        zero = jnp.zeros_like(faces[0])
        second = faces[1] if len(faces) > 1 else zero
        low = jnp.where(even, second, faces[0])
        high = jnp.where(even, faces[0], second)
        low = jnp.where(index > 0, low, zero)
        high = jnp.where(index < count - 1, high, zero)
        ghosts[axis] = (low, high)
    return ghosts


def embed_z(pair, shape):
    nx, ny, nz = shape
    low, high = pair
    rows = jnp.concatenate([low, high, jnp.zeros((6, nx * ny), F32)], axis=0)
    lane = jnp.where(iota((8, nz), 0) == 0, 0, nz - 1)
    pick = ((iota((8, nz), 1) == lane) & (iota((8, nz), 0) < 2)).astype(F32)
    return dot(rows, pick, 0, 0, HIGH).reshape(shape)


def interior(t, c):
    shape = t.shape
    nx, ny, nz = shape
    gain = jnp.zeros(shape, F32)
    weight = jnp.zeros(shape, F32)
    wx = 0.5 * (c[:-1] + c[1:])
    none = jnp.zeros((1, ny, nz), F32)
    w_low = jnp.concatenate([none, wx], axis=0)
    w_high = jnp.concatenate([wx, none], axis=0)
    t_low = jnp.concatenate([none, t[:-1]], axis=0)
    t_high = jnp.concatenate([t[1:], none], axis=0)
    gain = gain + w_low * t_low + w_high * t_high
    weight = weight + w_low + w_high
    for dim, n in ((1, ny), (2, nz)):
        at = iota(shape, dim)
        for shift, edge in ((1, 0), (n - 1, n - 1)):
            w = jnp.where(at == edge, 0.0, 0.5 * (c + pltpu.roll(c, shift, dim)))
            gain = gain + w * pltpu.roll(t, shift, dim)
            weight = weight + w
    return gain, weight


def shards(
    initial_hydraulic_head,
    well_discharge,
    local_facet_coupling,
    diagonal_capacity,
    crossing_permeability,
    crossing_partner_number,
    liquid_thermal_state,
    transfer_factor,
    host_voxel_number,
    stone_thermal_state,
    matrix_diffusivity,
):
    nb, links = crossing_partner_number.shape
    tri = initial_hydraulic_head.shape[1]
    shape = stone_thermal_state.shape
    nx, ny, nz = shape
    rows_n = nx * ny
    n = group_size()
    pairs = by_pairs()
    specs2 = face_specs(shape, 2)
    specs1 = face_specs(shape, 1)
    nf = len(specs1)
    blk = sds((nb, tri))
    slab = sds(shape)

    def prep(ids_ref, perm_ref, diag_ref, mix_ref, den_ref):
        me = lax.axis_index("gx") * lax.axis_size("gy") + lax.axis_index("gy")
        ids, perm = ids_ref[...], perm_ref[...]
        if pairs:
            ids = ids ^ (me * nb)
        at = iota((nb, n * nb), 1)
        mix = jnp.zeros((nb, n * nb), F32)
        den = jnp.zeros((nb, 1), F32)
        for k in range(links):
            mix = mix + jnp.where(at == ids[:, k : k + 1], perm[:, k : k + 1], 0.0)
            den = den + perm[:, k : k + 1]
        mix_ref[...] = mix
        den_ref[...] = diag_ref[...] + den

    def inner_body(a_ref, h_ref, o_ref):
        h = h_ref[...].astype(BF16)
        for b in range(nb):
            o_ref[b : b + 1, :] = dot(h[b : b + 1, :], a_ref[b], 1, 1)

    def inner_of(h):
        return call(inner_body, blk, local_facet_coupling, h, name="inner")

    def sweep_of(mix_ref, den_ref, w_ref, inner_ref, slot_refs):
        heads = [r[...] for r in slot_refs]
        heads = jnp.concatenate(heads, axis=0) if len(heads) > 1 else heads[0]
        across = dot(mix_ref[...], heads, 1, 0, HIGH)
        return (w_ref[...] + inner_ref[...] + across) / den_ref[...]

    def sweep(mix_ref, den_ref, w_ref, inner_ref, *rest):
        rest[-1][...] = sweep_of(mix_ref, den_ref, w_ref, inner_ref, rest[:-1])

    def send_first(t_ref, c_ref, *outs):
        write_faces(outs, specs2, (t_ref[...], c_ref[...]))

    def gather(t_ref, hv_ref, liq_ref, tf_ref, q_ref, hot_ref):
        t = t_ref[...].reshape(rows_n, nz)
        hi = t.astype(BF16)
        lo = (t - hi.astype(F32)).astype(BF16)
        both = jnp.concatenate([hi, lo], axis=1)
        hv = hv_ref[...]
        step = 4
        for b in range(0, nb, step):
            cell = jnp.concatenate([hv[i : i + 1, :] for i in range(b, b + step)], axis=1)
            width = step * tri
            hot = (iota((rows_n, width), 0) == cell // nz).astype(F32).astype(BF16)
            hot_ref[:, b * tri : b * tri + width] = hot
            rows = dot(both, hot, 0, 0)
            rows = rows[:nz] + rows[nz:]
            value = jnp.sum(jnp.where(iota((nz, width), 0) == cell % nz, rows, 0.0), axis=0, keepdims=True)
            for i in range(step):
                q_ref[b + i : b + i + 1, :] = value[:, i * tri : (i + 1) * tri]
        q_ref[...] = tf_ref[...] * (liq_ref[...] - q_ref[...])

    def base(t_ref, c_ref, *rest):
        got, outs = rest[:nf], rest[nf:]
        u_ref, keep_ref, wx_ref, wy_ref, wz_ref = outs
        t, c = t_ref[...], c_ref[...]
        gt = read_ghosts(got, specs2, 0)
        gc = read_ghosts(got, specs2, 1)
        gain, weight = interior(t, c)
        zx = jnp.zeros((ny, nz), F32)
        zy = jnp.zeros((nx, nz), F32)
        cx = gc["gx"] or (zx, zx)
        cy = gc["gy"] or (zy, zy)
        wx_low, wx_high = 0.5 * (c[0] + cx[0]), 0.5 * (c[nx - 1] + cx[1])
        wy_low, wy_high = 0.5 * (c[:, 0, :] + cy[0]), 0.5 * (c[:, ny - 1, :] + cy[1])
        at = iota(shape, 2)
        cz = embed_z(gc["gz"], shape) if gc["gz"] else jnp.zeros(shape, F32)
        wz = jnp.where((at == 0) | (at == nz - 1), 0.5 * (c + cz), 0.0)
        wx_ref[0], wx_ref[1] = wx_low, wx_high
        wy_ref[0], wy_ref[1] = wy_low, wy_high
        wz_ref[...] = wz
        keep_ref[...] = 1.0 - weight - wz
        keep_ref[0] = keep_ref[0] - wx_low
        keep_ref[nx - 1] = keep_ref[nx - 1] - wx_high
        keep_ref[:, 0, :] = keep_ref[:, 0, :] - wy_low
        keep_ref[:, ny - 1, :] = keep_ref[:, ny - 1, :] - wy_high
        u_ref[...] = gain + t * keep_ref[...]
        add_ghosts(u_ref, gt, wx_ref, wy_ref, wz_ref)

    def add_ghosts(u_ref, ghosts, wx_ref, wy_ref, wz_ref):
        if ghosts["gz"]:
            u_ref[...] = u_ref[...] + wz_ref[...] * embed_z(ghosts["gz"], shape)
        if ghosts["gx"]:
            u_ref[0] = u_ref[0] + wx_ref[0] * ghosts["gx"][0]
            u_ref[nx - 1] = u_ref[nx - 1] + wx_ref[1] * ghosts["gx"][1]
        if ghosts["gy"]:
            u_ref[:, 0, :] = u_ref[:, 0, :] + wy_ref[0] * ghosts["gy"][0]
            u_ref[:, ny - 1, :] = u_ref[:, ny - 1, :] + wy_ref[1] * ghosts["gy"][1]

    def heat(mix_ref, den_ref, w_ref, inner_ref, q_ref, hv_ref, hot_ref, u_ref, *rest):
        ns = len(rest) - 3 - nf - 1
        slots, outs, pick_ref = rest[:ns], rest[ns:-1], rest[-1]
        h_ref, f_ref, t_ref = outs[:3]
        h = sweep_of(mix_ref, den_ref, w_ref, inner_ref, slots)
        h_ref[...] = h
        flux = q_ref[...] * jnp.sqrt(1.0 + h * h)
        hi = flux.astype(BF16).astype(F32)
        lo = flux - hi
        lane = hv_ref[...] % nz
        for b in range(nb):
            mask = iota((nz, tri), 0) == lane[b : b + 1, :]
            pick_ref[:nz, b * tri : (b + 1) * tri] = jnp.where(mask, hi[b : b + 1, :], 0.0).astype(BF16)
            pick_ref[nz:, b * tri : (b + 1) * tri] = jnp.where(mask, lo[b : b + 1, :], 0.0).astype(BF16)
        both = dot(hot_ref[...], pick_ref[...], 1, 1)
        f = (both[:, :nz] + both[:, nz:]).reshape(shape)
        f_ref[...] = f
        t = u_ref[...] + f
        t_ref[...] = t
        write_faces(outs[3:], specs1, (t,))

    def middle(t_ref, f_ref, c_ref, keep_ref, v_ref):
        t = t_ref[...]
        gain, _ = interior(t, c_ref[...])
        v_ref[...] = f_ref[...] + t * keep_ref[...] + gain

    def last(v_ref, wx_ref, wy_ref, wz_ref, *rest):
        got, o_ref = rest[:-1], rest[-1]
        o_ref[...] = v_ref[...]
        add_ghosts(o_ref, read_ghosts(got, specs1, 0), wx_ref, wy_ref, wz_ref)

    h = initial_hydraulic_head
    slots = meet(h)
    faces = call(send_first, [sds(s) for _, _, s in specs2], stone_thermal_state, matrix_diffusivity, name="send_first")
    got = exchange(faces, specs2)
    mix, den = call(prep, (sds((nb, n * nb)), blk), crossing_partner_number, crossing_permeability, diagonal_capacity, name="prep")
    inner = inner_of(h)
    h = call(sweep, blk, mix, den, well_discharge, inner, *slots, name="sweep")
    q, hot = call(
        gather,
        (blk, sds((rows_n, nb * tri), BF16)),
        stone_thermal_state,
        host_voxel_number,
        liquid_thermal_state,
        transfer_factor,
        name="gather",
    )
    u, keep, wx, wy, wz = call(
        base,
        (slab, slab, sds((2, ny, nz)), sds((2, nx, nz)), slab),
        stone_thermal_state,
        matrix_diffusivity,
        *got,
        name="base",
    )
    for _ in range(SWEEPS - 2):
        slots = meet(h)
        inner = inner_of(h)
        h = call(sweep, blk, mix, den, well_discharge, inner, *slots, name="sweep")
    slots = meet(h)
    inner = inner_of(h)
    h, f, t, *faces = call(
        heat,
        [blk, slab, slab] + [sds(s) for _, _, s in specs1],
        mix,
        den,
        well_discharge,
        inner,
        q,
        host_voxel_number,
        hot,
        u,
        *slots,
        scratch=[pltpu.VMEM((2 * nz, nb * tri), BF16)],
        name="heat",
    )
    got = exchange(faces, specs1)
    v = call(middle, slab, t, f, matrix_diffusivity, keep, name="middle")
    out = call(last, slab, v, wx, wy, wz, *got, name="last")
    return (h, out)


def solution(mesh):
    block = P(AXES, None)
    rock = P(*AXES)
    in_specs = (block, block, P(AXES, None, None)) + (block,) * 6 + (rock, rock)
    return jax.shard_map(shards, mesh=mesh, in_specs=in_specs, out_specs=(block, rock), check_vma=False)
```

```python
import functools

import jax
import jax.numpy as jnp
from jax import lax
from jax.experimental import pallas as pl
from jax.experimental.pallas import tpu as pltpu
from jax.sharding import PartitionSpec as P


SWEEPS = 3
AXES = ("gx", "gy", "gz")
GROUP = ("gx", "gy")
F32 = jnp.float32
BF16 = jnp.bfloat16
HIGH = lax.Precision.HIGHEST


def call(body, out_shape, *args, scratch=(), hbm=0):
    vmem = pl.BlockSpec(memory_space=pltpu.VMEM)
    args = [pltpu.with_memory_space_constraint(x, pltpu.HBM) for x in args[:hbm]] + list(args[hbm:])
    return pl.pallas_call(
        body,
        out_shape=out_shape,
        in_specs=[pl.BlockSpec(memory_space=pltpu.HBM)] * hbm + [vmem] * (len(args) - hbm),
        scratch_shapes=scratch,
        compiler_params=pltpu.CompilerParams(vmem_limit_bytes=48 << 20),
    )(*args)


def sds(shape, dtype=F32):
    return jax.ShapeDtypeStruct(shape, dtype)


def iota(shape, dim):
    return lax.broadcasted_iota(jnp.int32, shape, dim)


def dot(a, b, ca, cb, precision=None):
    return lax.dot_general(
        a, b, (((ca,), (cb,)), ((), ())), precision=precision, preferred_element_type=F32
    )


def group_size():
    return lax.axis_size("gx") * lax.axis_size("gy")


def by_pairs():
    n = group_size()
    return n <= 8 and n & (n - 1) == 0 and lax.axis_size("gx") % 2 == 0


def swap(x, k):
    n = group_size()
    return lax.ppermute(x, GROUP, [(i, i ^ k) for i in range(n)])


def meet(x):
    if not by_pairs():
        return [lax.all_gather(x, GROUP, axis=0, tiled=True)]
    n = group_size()
    low = lax.axis_size("gy")
    slots = [None] * n
    slots[0] = x
    for k in range(n - 1, 0, -1):
        if not k & low:
            slots[k] = swap(x, k)
    for k in range(n):
        if not k & low:
            slots[k | low] = swap(slots[k], low)
    return slots


def pair_lists(count):
    first = [(i, i ^ 1 if (i ^ 1) < count else i) for i in range(count)]
    second = []
    for i in range(count):
        j = i + 1 if i % 2 else i - 1
        second.append((i, j if 0 <= j < count else i))
    return first, second


def rounds_of(axis):
    count = lax.axis_size(axis)
    return 0 if count == 1 else 1 if count == 2 else 2


def face_specs(shape, lead):
    nx, ny, nz = shape
    full = {"gx": (lead, ny, nz), "gy": (lead, nx, nz), "gz": (lead, nx * ny)}
    return [(axis, r, full[axis]) for axis in AXES for r in range(rounds_of(axis))]


def exchange(faces, specs):
    out = []
    for face, (axis, r, _) in zip(faces, specs):
        out.append(lax.ppermute(face, axis, pair_lists(lax.axis_size(axis))[r]))
    return out


def write_faces(refs, specs, fields):
    for ref, (axis, r, _) in zip(refs, specs):
        even = lax.axis_index(axis) % 2 == 0
        high = even if r == 0 else jnp.logical_not(even)
        for j, t in enumerate(fields):
            nx, ny, nz = t.shape
            if axis == "gx":
                ref[j] = jnp.where(high, t[nx - 1], t[0])
            elif axis == "gy":
                ref[j] = jnp.where(high, t[:, ny - 1, :], t[:, 0, :])
            else:
                lane = jnp.where(high, nz - 1, 0)
                pick = (iota((8, nz), 1) == lane).astype(F32)
                row = dot(pick, t.reshape(nx * ny, nz), 1, 1, HIGH)
                ref[j : j + 1, :] = row[0:1, :]


def read_ghosts(refs, specs, j):
    got = {axis: [] for axis in AXES}
    for ref, (axis, r, _) in zip(refs, specs):
        got[axis].append(ref[j : j + 1, :] if axis == "gz" else ref[j])
    ghosts = {}
    for axis in AXES:
        faces = got[axis]
        if not faces:
            ghosts[axis] = None
            continue
        index, count = lax.axis_index(axis), lax.axis_size(axis)
        even = index % 2 == 0
        zero = jnp.zeros_like(faces[0])
        second = faces[1] if len(faces) > 1 else zero
        low = jnp.where(even, second, faces[0])
        high = jnp.where(even, faces[0], second)
        low = jnp.where(index > 0, low, zero)
        high = jnp.where(index < count - 1, high, zero)
        ghosts[axis] = (low, high)
    return ghosts


def embed_z(pair, shape):
    nx, ny, nz = shape
    low, high = pair
    rows = jnp.concatenate([low, high, jnp.zeros((6, nx * ny), F32)], axis=0)
    lane = jnp.where(iota((8, nz), 0) == 0, 0, nz - 1)
    pick = ((iota((8, nz), 1) == lane) & (iota((8, nz), 0) < 2)).astype(F32)
    return dot(rows, pick, 0, 0, HIGH).reshape(shape)


def interior(t, c):
    shape = t.shape
    _, ny, nz = shape
    gain = jnp.zeros(shape, F32)
    weight = jnp.zeros(shape, F32)
    wx = 0.5 * (c[:-1] + c[1:])
    none = jnp.zeros((1, ny, nz), F32)
    w_low = jnp.concatenate([none, wx], axis=0)
    w_high = jnp.concatenate([wx, none], axis=0)
    t_low = jnp.concatenate([none, t[:-1]], axis=0)
    t_high = jnp.concatenate([t[1:], none], axis=0)
    gain = gain + w_low * t_low + w_high * t_high
    weight = weight + w_low + w_high
    for dim, n in ((1, ny), (2, nz)):
        at = iota(shape, dim)
        for shift, edge in ((1, 0), (n - 1, n - 1)):
            w = jnp.where(at == edge, 0.0, 0.5 * (c + pltpu.roll(c, shift, dim)))
            gain = gain + w * pltpu.roll(t, shift, dim)
            weight = weight + w
    return gain, weight


def shards(
    initial_hydraulic_head,
    well_discharge,
    local_facet_coupling,
    diagonal_capacity,
    crossing_permeability,
    crossing_partner_number,
    liquid_thermal_state,
    transfer_factor,
    host_voxel_number,
    stone_thermal_state,
    matrix_diffusivity,
):
    nb, links = crossing_partner_number.shape
    tri = initial_hydraulic_head.shape[1]
    shape = stone_thermal_state.shape
    nx, ny, nz = shape
    rows_n = nx * ny
    n = group_size()
    pairs = by_pairs()
    specs2 = face_specs(shape, 2)
    specs1 = face_specs(shape, 1)
    nf = len(specs1)
    blk = sds((nb, tri))
    slab = sds(shape)

    def pre(*refs):
        (ids_hbm, perm_hbm, diag_hbm, *hbm), refs = refs[:11], refs[11:]
        kept, refs = refs[: len(hbm)], refs[len(hbm) :]
        mix_ref, den_ref, inner_ref, *faces = refs[: 3 + nf]
        ids_ref, perm_ref, sems = refs[3 + nf :]
        copies = [
            pltpu.make_async_copy(src, dst, sems.at[i])
            for i, (src, dst) in enumerate(
                zip((ids_hbm, perm_hbm, diag_hbm, *hbm), (ids_ref, perm_ref, den_ref, *kept))
            )
        ]
        for copy in copies:
            copy.start()
        h_ref, a_ref, t_ref, c_ref = kept[:4]
        for copy in copies[:3]:
            copy.wait()
        me = lax.axis_index("gx") * lax.axis_size("gy") + lax.axis_index("gy")
        ids, perm = ids_ref[...], perm_ref[...]
        if pairs:
            ids = ids ^ (me * nb)
        at = iota((n * nb, nb), 0)
        mix = jnp.zeros((n * nb, nb), F32)
        for k in range(links):
            mix = mix + jnp.where(at == ids[k : k + 1, :], perm[k : k + 1, :], 0.0)
        mix_ref[...] = mix
        rows = jnp.concatenate([perm, jnp.zeros((-links % 8, nb), F32)], axis=0)
        den_ref[...] = den_ref[...] + dot(rows, jnp.ones((rows.shape[0], tri), F32), 0, 0, HIGH)
        copies[3].wait()
        copies[4].wait()
        inner_body(a_ref, h_ref, inner_ref)
        for copy in copies[5:]:
            copy.wait()
        write_faces(faces, specs2, (t_ref[...], c_ref[...]))

    def inner_body(a_ref, h_ref, o_ref):
        h = h_ref[...].astype(BF16)
        for b in range(nb):
            o_ref[b : b + 1, :] = dot(h[b : b + 1, :], a_ref[b], 1, 1)

    def inner_of(h):
        return call(inner_body, blk, a, h)

    def sweep_of(mix_ref, den_ref, w_ref, inner_ref, slot_refs):
        heads = [r[...] for r in slot_refs]
        heads = jnp.concatenate(heads, axis=0) if len(heads) > 1 else heads[0]
        across = dot(mix_ref[...], heads, 0, 0, HIGH)
        return (w_ref[...] + inner_ref[...] + across) / den_ref[...]

    def sweep(mix_ref, den_ref, w_ref, inner_ref, *rest):
        rest[-1][...] = sweep_of(mix_ref, den_ref, w_ref, inner_ref, rest[:-1])

    def gather(first, t_ref, hv_ref, liq_ref, tf_ref, q_ref, hot_ref):
        t = t_ref[...].reshape(rows_n, nz)
        hi = t.astype(BF16)
        lo = (t - hi.astype(F32)).astype(BF16)
        both = jnp.concatenate([hi, lo], axis=1)
        hv = hv_ref[...]
        step = 4
        half = hot_ref.shape[1] // tri
        for b in range(0, half, step):
            cell = jnp.concatenate([hv[first + i : first + i + 1, :] for i in range(b, b + step)], axis=1)
            width = step * tri
            hot = (iota((rows_n, width), 0) == cell // nz).astype(F32).astype(BF16)
            hot_ref[:, b * tri : b * tri + width] = hot
            rows = dot(both, hot, 0, 0)
            rows = rows[:nz] + rows[nz:]
            value = jnp.sum(jnp.where(iota((nz, width), 0) == cell % nz, rows, 0.0), axis=0, keepdims=True)
            for i in range(step):
                q_ref[b + i : b + i + 1, :] = value[:, i * tri : (i + 1) * tri]
        own = slice(first, first + half)
        q_ref[...] = tf_ref[own, :] * (liq_ref[own, :] - q_ref[...])

    def base(t_ref, c_ref, *rest):
        got, outs = rest[:nf], rest[nf:]
        u_ref, keep_ref, wx_ref, wy_ref, wz_ref = outs
        t, c = t_ref[...], c_ref[...]
        gt = read_ghosts(got, specs2, 0)
        gc = read_ghosts(got, specs2, 1)
        gain, weight = interior(t, c)
        zx = jnp.zeros((ny, nz), F32)
        zy = jnp.zeros((nx, nz), F32)
        cx = gc["gx"] or (zx, zx)
        cy = gc["gy"] or (zy, zy)
        wx_low, wx_high = 0.5 * (c[0] + cx[0]), 0.5 * (c[nx - 1] + cx[1])
        wy_low, wy_high = 0.5 * (c[:, 0, :] + cy[0]), 0.5 * (c[:, ny - 1, :] + cy[1])
        at = iota(shape, 2)
        cz = embed_z(gc["gz"], shape) if gc["gz"] else jnp.zeros(shape, F32)
        wz = jnp.where((at == 0) | (at == nz - 1), 0.5 * (c + cz), 0.0)
        wx_ref[0], wx_ref[1] = wx_low, wx_high
        wy_ref[0], wy_ref[1] = wy_low, wy_high
        wz_ref[...] = wz
        keep_ref[...] = 1.0 - weight - wz
        keep_ref[0] = keep_ref[0] - wx_low
        keep_ref[nx - 1] = keep_ref[nx - 1] - wx_high
        keep_ref[:, 0, :] = keep_ref[:, 0, :] - wy_low
        keep_ref[:, ny - 1, :] = keep_ref[:, ny - 1, :] - wy_high
        u_ref[...] = gain + t * keep_ref[...]
        add_ghosts(u_ref, gt, wx_ref, wy_ref, wz_ref)

    def add_ghosts(u_ref, ghosts, wx_ref, wy_ref, wz_ref):
        if ghosts["gz"]:
            u_ref[...] = u_ref[...] + wz_ref[...] * embed_z(ghosts["gz"], shape)
        if ghosts["gx"]:
            u_ref[0] = u_ref[0] + wx_ref[0] * ghosts["gx"][0]
            u_ref[nx - 1] = u_ref[nx - 1] + wx_ref[1] * ghosts["gx"][1]
        if ghosts["gy"]:
            u_ref[:, 0, :] = u_ref[:, 0, :] + wy_ref[0] * ghosts["gy"][0]
            u_ref[:, ny - 1, :] = u_ref[:, ny - 1, :] + wy_ref[1] * ghosts["gy"][1]

    def heat(mix_ref, den_ref, w_ref, inner_ref, q1_ref, q2_ref, hv_ref, hot1_ref, hot2_ref, u_ref, *rest):
        ns = len(rest) - 3 - nf - 1
        slots, outs, pick_ref = rest[:ns], rest[ns:-1], rest[-1]
        h_ref, f_ref, t_ref = outs[:3]
        h = sweep_of(mix_ref, den_ref, w_ref, inner_ref, slots)
        h_ref[...] = h
        q = jnp.concatenate([q1_ref[...], q2_ref[...]], axis=0)
        flux = q * jnp.sqrt(1.0 + h * h)
        hi = flux.astype(BF16).astype(F32)
        lo = flux - hi
        lane = hv_ref[...] % nz
        for b in range(nb):
            mask = iota((nz, tri), 0) == lane[b : b + 1, :]
            pick_ref[:nz, b * tri : (b + 1) * tri] = jnp.where(mask, hi[b : b + 1, :], 0.0).astype(BF16)
            pick_ref[nz:, b * tri : (b + 1) * tri] = jnp.where(mask, lo[b : b + 1, :], 0.0).astype(BF16)
        half = hot1_ref.shape[1]
        both = dot(hot1_ref[...], pick_ref[:, :half], 1, 1) + dot(hot2_ref[...], pick_ref[:, half:], 1, 1)
        f = (both[:, :nz] + both[:, nz:]).reshape(shape)
        f_ref[...] = f
        t = u_ref[...] + f
        t_ref[...] = t
        write_faces(outs[3:], specs1, (t,))

    def middle(t_ref, f_ref, c_ref, keep_ref, v_ref):
        t = t_ref[...]
        gain, _ = interior(t, c_ref[...])
        v_ref[...] = f_ref[...] + t * keep_ref[...] + gain

    def last(v_ref, wx_ref, wy_ref, wz_ref, *rest):
        got, o_ref = rest[:-1], rest[-1]
        o_ref[...] = v_ref[...]
        add_ghosts(o_ref, read_ghosts(got, specs1, 0), wx_ref, wy_ref, wz_ref)

    h = initial_hydraulic_head
    slots = meet(h)
    h, a, t, c, w, hv, liq, tf, mix, den, inner, *faces = call(
        pre,
        [blk, sds(local_facet_coupling.shape, BF16), slab, slab, blk, sds((nb, tri), jnp.int32), blk, blk]
        + [sds((n * nb, nb)), blk, blk]
        + [sds(s) for _, _, s in specs2],
        crossing_partner_number.T,
        crossing_permeability.T,
        diagonal_capacity,
        h,
        local_facet_coupling,
        stone_thermal_state,
        matrix_diffusivity,
        well_discharge,
        host_voxel_number,
        liquid_thermal_state,
        transfer_factor,
        scratch=[pltpu.VMEM((links, nb), jnp.int32), pltpu.VMEM((links, nb), F32), pltpu.SemaphoreType.DMA((11,))],
        hbm=11,
    )
    slots[0] = h if pairs else slots[0]
    got = exchange(faces, specs2)
    h = call(sweep, blk, mix, den, w, inner, *slots)
    half = nb // 2
    parts = []
    for i in range(2):
        parts.append(
            call(
                functools.partial(gather, i * half), (sds((half, tri)), sds((rows_n, half * tri), BF16)), t, hv, liq, tf
            )
        )
    (q1, hot1), (q2, hot2) = parts
    u, keep, wx, wy, wz = call(base, (slab, slab, sds((2, ny, nz)), sds((2, nx, nz)), slab), t, c, *got)
    for _ in range(SWEEPS - 2):
        slots = meet(h)
        inner = inner_of(h)
        h = call(sweep, blk, mix, den, w, inner, *slots)
    slots = meet(h)
    inner = inner_of(h)
    h, f, t, *faces = call(
        heat,
        [blk, slab, slab] + [sds(s) for _, _, s in specs1],
        mix,
        den,
        w,
        inner,
        q1,
        q2,
        hv,
        hot1,
        hot2,
        u,
        *slots,
        scratch=[pltpu.VMEM((2 * nz, nb * tri), BF16)],
    )
    got = exchange(faces, specs1)
    v = call(middle, slab, t, f, c, keep)
    out = call(last, slab, v, wx, wy, wz, *got)
    return (h, out)


def solution(mesh):
    block = P(AXES, None)
    rock = P(*AXES)
    in_specs = (block, block, P(AXES, None, None)) + (block,) * 6 + (rock, rock)

    return jax.shard_map(shards, mesh=mesh, in_specs=in_specs, out_specs=(block, rock), check_vma=False)
```

```python
import functools

import jax
import jax.numpy as jnp
from jax import lax
from jax.experimental import pallas as pl
from jax.experimental.pallas import tpu as pltpu
from jax.sharding import PartitionSpec as P


SWEEPS = 3
AXES = ("gx", "gy", "gz")
GROUP = ("gx", "gy")
F32 = jnp.float32
BF16 = jnp.bfloat16
HIGH = lax.Precision.HIGHEST


def call(body, out_shape, *args, scratch=(), hbm=0):
    vmem = pl.BlockSpec(memory_space=pltpu.VMEM)
    args = [pltpu.with_memory_space_constraint(x, pltpu.HBM) for x in args[:hbm]] + list(args[hbm:])
    return pl.pallas_call(
        body,
        out_shape=out_shape,
        in_specs=[pl.BlockSpec(memory_space=pltpu.HBM)] * hbm + [vmem] * (len(args) - hbm),
        scratch_shapes=scratch,
        compiler_params=pltpu.CompilerParams(vmem_limit_bytes=48 << 20),
    )(*args)


def sds(shape, dtype=F32):
    return jax.ShapeDtypeStruct(shape, dtype)


def iota(shape, dim):
    return lax.broadcasted_iota(jnp.int32, shape, dim)


def dot(a, b, ca, cb, precision=None):
    return lax.dot_general(
        a, b, (((ca,), (cb,)), ((), ())), precision=precision, preferred_element_type=F32
    )


def group_size():
    return lax.axis_size("gx") * lax.axis_size("gy")


def by_pairs():
    return lax.axis_size("gx") == 4 and lax.axis_size("gy") == 2


def swap(x, k):
    n = group_size()
    return lax.ppermute(x, GROUP, [(i, i ^ k) for i in range(n)])


def meet(direct, own):
    low = lax.axis_size("gy")
    slots = {k: swap(x, k) for k, x in direct.items()}
    slots[low] = swap(own, low)
    for k in direct:
        slots[k | low] = swap(slots[k], low)
    return slots


def pair_lists(count):
    first = [(i, i ^ 1 if (i ^ 1) < count else i) for i in range(count)]
    second = []
    for i in range(count):
        j = i + 1 if i % 2 else i - 1
        second.append((i, j if 0 <= j < count else i))
    return first, second


def rounds_of(axis):
    count = lax.axis_size(axis)
    return 0 if count == 1 else 1 if count == 2 else 2


def face_specs(shape, lead):
    nx, ny, nz = shape
    full = {"gx": (lead, ny, nz), "gy": (lead, nx, nz), "gz": (lead, nx * ny)}
    return [(axis, r, full[axis]) for axis in AXES for r in range(rounds_of(axis))]


def exchange(faces, specs):
    out = []
    for face, (axis, r, _) in zip(faces, specs):
        out.append(lax.ppermute(face, axis, pair_lists(lax.axis_size(axis))[r]))
    return out


def face_of(t, axis, r):
    nx, ny, nz = t.shape
    even = lax.axis_index(axis) % 2 == 0
    high = even if r == 0 else jnp.logical_not(even)
    if axis == "gx":
        return jnp.where(high, t[nx - 1], t[0])
    if axis == "gy":
        return jnp.where(high, t[:, ny - 1, :], t[:, 0, :])
    lane = jnp.where(high, nz - 1, 0)
    pick = (iota((8, nz), 1) == lane).astype(F32)
    return dot(pick, t.reshape(nx * ny, nz), 1, 1, HIGH)[0:1, :]


def write_faces(refs, specs, fields):
    for ref, (axis, r, _) in zip(refs, specs):
        for j, t in enumerate(fields):
            face = face_of(t, axis, r)
            if axis == "gz":
                ref[j : j + 1, :] = face
            else:
                ref[j] = face


def read_faces(refs, specs, j):
    got = {axis: [] for axis in AXES}
    for ref, (axis, r, _) in zip(refs, specs):
        got[axis].append(ref[j : j + 1, :] if axis == "gz" else ref[j])
    return got


def ghosts_of(axis, faces, like):
    zero = jnp.zeros(like, F32)
    if not faces:
        return zero, zero
    index, count = lax.axis_index(axis), lax.axis_size(axis)
    even = index % 2 == 0
    second = faces[1] if len(faces) > 1 else zero
    low = jnp.where(even, second, faces[0])
    high = jnp.where(even, faces[0], second)
    return jnp.where(index > 0, low, zero), jnp.where(index < count - 1, high, zero)


def embed_z(pair, shape):
    nx, ny, nz = shape
    low, high = pair
    rows = jnp.concatenate([low, high, jnp.zeros((6, nx * ny), F32)], axis=0)
    lane = jnp.where(iota((8, nz), 0) == 0, 0, nz - 1)
    pick = ((iota((8, nz), 1) == lane) & (iota((8, nz), 0) < 2)).astype(F32)
    return dot(rows, pick, 0, 0, HIGH).reshape(shape)


def interior(t, c):
    shape = t.shape
    _, ny, nz = shape
    gain = jnp.zeros(shape, F32)
    weight = jnp.zeros(shape, F32)
    wx = 0.5 * (c[:-1] + c[1:])
    none = jnp.zeros((1, ny, nz), F32)
    w_low = jnp.concatenate([none, wx], axis=0)
    w_high = jnp.concatenate([wx, none], axis=0)
    t_low = jnp.concatenate([none, t[:-1]], axis=0)
    t_high = jnp.concatenate([t[1:], none], axis=0)
    gain = gain + w_low * t_low + w_high * t_high
    weight = weight + w_low + w_high
    for dim, n in ((1, ny), (2, nz)):
        at = iota(shape, dim)
        for shift, edge in ((1, 0), (n - 1, n - 1)):
            w = jnp.where(at == edge, 0.0, 0.5 * (c + pltpu.roll(c, shift, dim)))
            gain = gain + w * pltpu.roll(t, shift, dim)
            weight = weight + w
    return gain, weight


def shards(
    initial_hydraulic_head,
    well_discharge,
    local_facet_coupling,
    diagonal_capacity,
    crossing_permeability,
    crossing_partner_number,
    liquid_thermal_state,
    transfer_factor,
    host_voxel_number,
    stone_thermal_state,
    matrix_diffusivity,
):
    nb, links = crossing_partner_number.shape
    tri = initial_hydraulic_head.shape[1]
    shape = stone_thermal_state.shape
    nx, ny, nz = shape
    rows_n = nx * ny
    n = group_size()
    low = lax.axis_size("gy")
    pairs = by_pairs() and 4 * nb == tri
    specs2 = face_specs(shape, 2)
    specs1 = face_specs(shape, 1)
    xy = [i for i, spec in enumerate(specs2) if spec[0] != "gz"]
    zs = [i for i, spec in enumerate(specs2) if spec[0] == "gz"]
    blk = sds((nb, tri))
    slab = sds(shape)
    small = -(-2 * links // 8) * 8

    def load(copies):
        copies = [pltpu.make_async_copy(src, dst, sem) for src, dst, sem in copies]
        for copy in copies:
            copy.start()
        return copies

    def inner_of(a_ref, h):
        h = h.astype(BF16)
        return jnp.concatenate([dot(h[b : b + 1, :], a_ref[b], 1, 1) for b in range(nb)], axis=0)

    def mix_of(ids, perm):
        at = iota((n * nb, ids.shape[1]), 0)
        mix = jnp.zeros(at.shape, F32)
        for k in range(links):
            mix = mix + jnp.where(at == ids[k : k + 1, :], perm[k : k + 1, :], 0.0)
        return mix

    def pre(ids_hbm, perm_hbm, diag_hbm, h_hbm, w_hbm, a_hbm, send_ref, w_ref, a_ref, ids_ref, perm_ref, den_ref, h_ref, sems):
        pieces = ((ids_hbm, ids_ref), (perm_hbm, perm_ref), (diag_hbm, den_ref), (h_hbm, h_ref), (w_hbm, w_ref), (a_hbm, a_ref))
        copies = load([(src, dst, sems.at[i]) for i, (src, dst) in enumerate(pieces)])
        send_ref[3 * nb :, :] = jnp.zeros((small, tri), F32)
        for copy in copies[:5]:
            copy.wait()
        perm = perm_ref[...]
        send_ref[3 * nb : 3 * nb + links, :nb] = ids_ref[...].astype(F32)
        send_ref[3 * nb + links : 3 * nb + 2 * links, :nb] = perm
        rows = jnp.concatenate([perm, jnp.zeros((-links % 8, nb), F32)], axis=0)
        send_ref[2 * nb : 3 * nb, :] = den_ref[...] + dot(rows, jnp.ones((rows.shape[0], tri), F32), 0, 0, HIGH)
        h = h_ref[...]
        send_ref[:nb, :] = h
        copies[5].wait()
        send_ref[nb : 2 * nb, :] = w_ref[...] + inner_of(a_ref, h)

    def rock(*refs):
        nf = len(specs2)
        hbm, kept, faces, sems = refs[:5], refs[5:10], refs[10 : 10 + nf], refs[-1]
        copies = load([(src, dst, sems.at[i]) for i, (src, dst) in enumerate(zip(hbm, kept))])
        for copy in copies:
            copy.wait()
        write_faces(faces, specs2, (kept[0][...], kept[1][...]))

    def both(w_ref, a_ref, *rest):
        slots, rest = rest[:n], rest[n:]
        faces, (h_ref, mix_ref, *sends) = rest[: len(xy)], rest[len(xy) :]
        me = lax.axis_index("gx") * low + lax.axis_index("gy")
        heads = jnp.concatenate([s[:nb, :] for s in slots], axis=0)
        per = tri // nb
        first = []
        for g in range(0, n, per):
            table = slots[g][3 * nb :, :]
            for i in range(1, per):
                table = table + pltpu.roll(slots[g + i][3 * nb :, :], i * nb, 1)
            ids = table[:links, :].astype(jnp.int32) ^ (me * nb)
            mix = mix_of(ids, table[links : 2 * links, :])
            if g == 0:
                mix_ref[...] = mix
            across = dot(mix, heads, 0, 0, HIGH)
            for i in range(per):
                s = slots[g + i]
                first.append((s[nb : 2 * nb, :] + across[i * nb : (i + 1) * nb, :]) / s[2 * nb : 3 * nb, :])
        inner = inner_of(a_ref, first[0])
        across = dot(mix_ref[...], jnp.concatenate(first, axis=0), 0, 0, HIGH)[:nb, :]
        h = (w_ref[...] + inner + across) / slots[0][2 * nb : 3 * nb, :]
        h_ref[...] = h
        for send, face in zip(sends, faces):
            send[:nb, :] = h
            half = face.shape[1]
            send[nb : nb + half, :] = face[0]
            send[nb + half : nb + 2 * half, :] = face[1]

    def inner_body(a_ref, h_ref, o_ref):
        o_ref[...] = inner_of(a_ref, h_ref[...])

    def sweep(w_ref, den_ref, mix_ref, inner_ref, heads):
        across = dot(mix_ref[...], heads, 0, 0, HIGH)[:nb, :]
        return (w_ref[...] + inner_ref[...] + across) / den_ref[...]

    def gather(first, t_ref, hv_ref, liq_ref, tf_ref, q_ref, hot_ref):
        t = t_ref[...].reshape(rows_n, nz)
        hi = t.astype(BF16)
        lo = (t - hi.astype(F32)).astype(BF16)
        parts = jnp.concatenate([hi, lo], axis=1)
        hv = hv_ref[...]
        step = 4
        half = hot_ref.shape[1] // tri
        for b in range(0, half, step):
            cell = jnp.concatenate([hv[first + i : first + i + 1, :] for i in range(b, b + step)], axis=1)
            width = step * tri
            hot = (iota((rows_n, width), 0) == cell // nz).astype(F32).astype(BF16)
            hot_ref[:, b * tri : b * tri + width] = hot
            rows = dot(parts, hot, 0, 0)
            rows = rows[:nz] + rows[nz:]
            value = jnp.sum(jnp.where(iota((nz, width), 0) == cell % nz, rows, 0.0), axis=0, keepdims=True)
            for i in range(step):
                q_ref[b + i : b + i + 1, :] = value[:, i * tri : (i + 1) * tri]
        own = slice(first, first + half)
        q_ref[...] = tf_ref[own, :] * (liq_ref[own, :] - q_ref[...])

    def base(t_ref, c_ref, *rest):
        got, (u_ref, keep_ref, wz_ref) = rest[: len(zs)], rest[len(zs) :]
        specs = [specs2[i] for i in zs]
        t, c = t_ref[...], c_ref[...]
        tz = ghosts_of("gz", read_faces(got, specs, 0)["gz"], (1, rows_n))
        cz = ghosts_of("gz", read_faces(got, specs, 1)["gz"], (1, rows_n))
        gain, weight = interior(t, c)
        at = iota(shape, 2)
        wz = jnp.where((at == 0) | (at == nz - 1), 0.5 * (c + embed_z(cz, shape)), 0.0)
        keep = 1.0 - weight - wz
        wz_ref[...] = wz
        keep_ref[...] = keep
        u_ref[...] = gain + t * keep + wz * embed_z(tz, shape)

    def add_sides(u_ref, t_ref, wx_ref, wy_ref, gx, gy):
        for i, at in enumerate((0, nx - 1)):
            u_ref[at] = u_ref[at] + wx_ref[i] * (gx[i] - t_ref[at])
        for i, at in enumerate((0, ny - 1)):
            u_ref[:, at, :] = u_ref[:, at, :] + wy_ref[i] * (gy[i] - t_ref[:, at, :])

    def heat(get_sides, get_heads, ns, *refs):
        mix_ref, den_ref, w_ref, inner_ref, q1_ref, q2_ref, hv_ref, hot1_ref, hot2_ref, u_ref, t0_ref, c_ref = refs[:12]
        got, rest = refs[12 : 12 + ns], refs[12 + ns :]
        h_ref, f_ref, t_ref, wx_ref, wy_ref, *faces = rest[:-1]
        pick_ref = rest[-1]
        h = sweep(w_ref, den_ref, mix_ref, inner_ref, get_heads(got))
        h_ref[...] = h
        q = jnp.concatenate([q1_ref[...], q2_ref[...]], axis=0)
        flux = q * jnp.sqrt(1.0 + h * h)
        hi = flux.astype(BF16).astype(F32)
        lo = flux - hi
        lane = hv_ref[...] % nz
        for b in range(nb):
            mask = iota((nz, tri), 0) == lane[b : b + 1, :]
            pick_ref[:nz, b * tri : (b + 1) * tri] = jnp.where(mask, hi[b : b + 1, :], 0.0).astype(BF16)
            pick_ref[nz:, b * tri : (b + 1) * tri] = jnp.where(mask, lo[b : b + 1, :], 0.0).astype(BF16)
        half = hot1_ref.shape[1]
        parts = dot(hot1_ref[...], pick_ref[:, :half], 1, 1) + dot(hot2_ref[...], pick_ref[:, half:], 1, 1)
        f = (parts[:, :nz] + parts[:, nz:]).reshape(shape)
        f_ref[...] = f
        t_ref[...] = u_ref[...] + f
        tx, ty = get_sides(got, 0)
        cx, cy = get_sides(got, 1)
        for i, at in enumerate((0, nx - 1)):
            wx_ref[i] = 0.5 * (c_ref[at] + cx[i])
        for i, at in enumerate((0, ny - 1)):
            wy_ref[i] = 0.5 * (c_ref[:, at, :] + cy[i])
        add_sides(t_ref, t0_ref, wx_ref, wy_ref, tx, ty)
        write_faces(faces, specs1, (t_ref[...],))

    def middle(t_ref, f_ref, c_ref, keep_ref, v_ref):
        t = t_ref[...]
        gain, _ = interior(t, c_ref[...])
        v_ref[...] = f_ref[...] + t * keep_ref[...] + gain

    def last(v_ref, t_ref, wx_ref, wy_ref, wz_ref, *rest):
        got, o_ref = rest[:-1], rest[-1]
        faces = read_faces(got, specs1, 0)
        o_ref[...] = v_ref[...] + wz_ref[...] * embed_z(ghosts_of("gz", faces["gz"], (1, rows_n)), shape)
        gx = ghosts_of("gx", faces["gx"], (ny, nz))
        gy = ghosts_of("gy", faces["gy"], (nx, nz))
        add_sides(o_ref, t_ref, wx_ref, wy_ref, gx, gy)

    send, w, a = call(
        pre,
        (sds((3 * nb + small, tri)), blk, sds(local_facet_coupling.shape, BF16)),
        crossing_partner_number.T,
        crossing_permeability.T,
        diagonal_capacity,
        initial_hydraulic_head,
        well_discharge,
        local_facet_coupling,
        scratch=[pltpu.VMEM((links, nb), jnp.int32), pltpu.VMEM((links, nb), F32)]
        + [pltpu.VMEM((nb, tri), F32)] * 2
        + [pltpu.SemaphoreType.DMA((6,))],
        hbm=6,
    )
    if pairs:
        slots = meet({k: send for k in range(n - 1, 0, -1) if not k & low}, send)
    t, c, hv, liq, tf, *faces = call(
        rock,
        [slab, slab, sds((nb, tri), jnp.int32), blk, blk] + [sds(s) for _, _, s in specs2],
        stone_thermal_state,
        matrix_diffusivity,
        host_voxel_number,
        liquid_thermal_state,
        transfer_factor,
        scratch=[pltpu.SemaphoreType.DMA((5,))],
        hbm=5,
    )
    got_z = exchange([faces[i] for i in zs], [specs2[i] for i in zs])
    if pairs:
        y_at, xa_at, xb_at = 1, low, 2 * low
        order = {"gx": (xa_at, xb_at), "gy": (y_at,)}
        rides = [order[specs2[i][0]][specs2[i][1]] for i in xy]
        h, mix, *sends = call(
            both,
            [blk, sds((n * nb, tri))] + [sds((nb + 2 * specs2[i][2][1], tri)) for i in xy],
            w,
            a,
            send,
            *[slots[k] for k in range(1, n)],
            *[faces[i] for i in xy],
        )
        ride = dict(zip(rides, sends))
        slots = meet({k: ride.get(k, h) for k in range(n - 1, 0, -1) if not k & low}, ride[low])
        den = send[2 * nb : 3 * nb]
        got = [h] + [slots[k] for k in range(1, n)]

        def get_heads(refs):
            return jnp.concatenate([r[:nb, :] for r in refs], axis=0)

        def get_sides(refs, j):
            x_rows, y_rows = slice(nb + j * ny, nb + (j + 1) * ny), slice(nb + j * nx, nb + (j + 1) * nx)
            gx = ghosts_of("gx", [refs[xa_at][x_rows, :], refs[xb_at | low][x_rows, :]], (ny, nz))
            return gx, ghosts_of("gy", [refs[y_at][y_rows, :]], (nx, nz))
    else:
        den = send[2 * nb : 3 * nb]
        h = initial_hydraulic_head
        ids = jnp.zeros((small, tri), jnp.int32).at[:links, :nb].set(crossing_partner_number.T)
        perm = send[3 * nb + links : 3 * nb + 2 * links]

        def mix_body(ids_ref, perm_ref, mix_ref):
            mix_ref[...] = mix_of(ids_ref[...], perm_ref[...])

        def sweep_body(w_ref, den_ref, mix_ref, inner_ref, heads_ref, h_ref):
            h_ref[...] = sweep(w_ref, den_ref, mix_ref, inner_ref, heads_ref[...])

        mix = call(mix_body, sds((n * nb, tri)), ids[:links], perm)
        for _ in range(SWEEPS - 1):
            heads = lax.all_gather(h, GROUP, axis=0, tiled=True)
            inner = call(inner_body, blk, a, h)
            h = call(sweep_body, blk, w, den, mix, inner, heads)
        got = [lax.all_gather(h, GROUP, axis=0, tiled=True)]
        got += exchange([faces[i] for i in xy], [specs2[i] for i in xy])

        def get_heads(refs):
            return refs[0][...]

        def get_sides(refs, j):
            sides = read_faces(refs[1:], [specs2[i] for i in xy], j)
            return ghosts_of("gx", sides["gx"], (ny, nz)), ghosts_of("gy", sides["gy"], (nx, nz))

    inner = call(inner_body, blk, a, h)
    half = nb // 2
    parts = [
        call(functools.partial(gather, i * half), (sds((half, tri)), sds((rows_n, half * tri), BF16)), t, hv, liq, tf)
        for i in range(2)
    ]
    (q1, hot1), (q2, hot2) = parts
    u, keep, wz = call(base, (slab, slab, slab), t, c, *got_z)
    h, f, t1, wx, wy, *faces = call(
        functools.partial(heat, get_sides, get_heads, len(got)),
        [blk, slab, slab, sds((2, ny, nz)), sds((2, nx, nz))] + [sds(s) for _, _, s in specs1],
        mix,
        den,
        w,
        inner,
        q1,
        q2,
        hv,
        hot1,
        hot2,
        u,
        t,
        c,
        *got,
        scratch=[pltpu.VMEM((2 * nz, nb * tri), BF16)],
    )
    got = exchange(faces, specs1)
    v = call(middle, slab, t1, f, c, keep)
    out = call(last, slab, v, t1, wx, wy, wz, *got)
    return (h, out)


def solution(mesh):
    block = P(AXES, None)
    rock = P(*AXES)
    in_specs = (block, block, P(AXES, None, None)) + (block,) * 6 + (rock, rock)

    return jax.shard_map(shards, mesh=mesh, in_specs=in_specs, out_specs=(block, rock), check_vma=False)
```

```python
import functools
import itertools

import jax
import jax.numpy as jnp
from jax import lax
from jax.experimental import pallas as pl
from jax.experimental.pallas import tpu as pltpu
from jax.sharding import PartitionSpec as P


SWEEPS = 3
AXES = ("gx", "gy", "gz")
GROUP = ("gx", "gy")
F32 = jnp.float32
BF16 = jnp.bfloat16
HIGH = lax.Precision.HIGHEST


def call(body, out_shape, *args, scratch=(), hbm=0):
    vmem = pl.BlockSpec(memory_space=pltpu.VMEM)
    args = [pltpu.with_memory_space_constraint(x, pltpu.HBM) for x in args[:hbm]] + list(args[hbm:])
    return pl.pallas_call(
        body,
        out_shape=out_shape,
        in_specs=[pl.BlockSpec(memory_space=pltpu.HBM)] * hbm + [vmem] * (len(args) - hbm),
        scratch_shapes=scratch,
        compiler_params=pltpu.CompilerParams(vmem_limit_bytes=48 << 20),
    )(*args)


def sds(shape, dtype=F32):
    return jax.ShapeDtypeStruct(shape, dtype)


def iota(shape, dim):
    return lax.broadcasted_iota(jnp.int32, shape, dim)


def dot(a, b, ca, cb, precision=None):
    return lax.dot_general(
        a, b, (((ca,), (cb,)), ((), ())), precision=precision, preferred_element_type=F32
    )


def group_size():
    return lax.axis_size("gx") * lax.axis_size("gy")


def by_pairs():
    return lax.axis_size("gx") == 4 and lax.axis_size("gy") == 2


def swap(x, k):
    n = group_size()
    return lax.ppermute(x, GROUP, [(i, i ^ k) for i in range(n)])


def meet(direct, own):
    low = lax.axis_size("gy")
    slots = {k: swap(x, k) for k, x in direct.items()}
    slots[low] = swap(own, low)
    for k in direct:
        slots[k | low] = swap(slots[k], low)
    return slots


def partner(axis, r, where):
    at, count, other = where[axis], lax.axis_size(axis), dict(where)
    up = at % 2 == r
    to = at + 1 if up else at - 1
    if 0 <= to < count:
        other[axis] = to
    elif axis == "gx":
        other[axis] = at if count % 2 else count - 1 - at
    elif lax.axis_size("gx") % 2 == 0:
        other["gx"] = where["gx"] ^ 1
    return other


def swap_list(axis, r):
    sizes = [lax.axis_size(a) for a in AXES]
    pairs = []
    for i, at in enumerate(itertools.product(*map(range, sizes))):
        other = partner(axis, r, dict(zip(AXES, at)))
        j = 0
        for a, size in zip(AXES, sizes):
            j = j * size + other[a]
        pairs.append((i, j))
    return pairs


def rounds_of(axis):
    count = lax.axis_size(axis)
    return 0 if count == 1 else 1 if count == 2 else 2


def face_specs(shape, lead):
    nx, ny, nz = shape
    full = {"gx": (lead, ny, nz), "gy": (lead, nx, nz), "gz": (lead, nx * ny)}
    return [(axis, r, full[axis]) for axis in AXES for r in range(rounds_of(axis))]


def exchange(faces, specs):
    out = []
    for face, (axis, r, _) in zip(faces, specs):
        out.append(lax.ppermute(face, AXES, swap_list(axis, r)))
    return out


def write_faces(refs, specs, fields):
    for j, t in enumerate(fields):
        nx, ny, nz = t.shape
        lanes = t.reshape(nx * ny, nz).T
        for ref, (axis, r, _) in zip(refs, specs):
            even = lax.axis_index(axis) % 2 == 0
            high = even if r == 0 else jnp.logical_not(even)
            if axis == "gx":
                ref[j] = jnp.where(high, t[nx - 1], t[0])
            elif axis == "gy":
                ref[j] = jnp.where(high, t[:, ny - 1, :], t[:, 0, :])
            else:
                ref[j : j + 1, :] = jnp.where(high, lanes[nz - 1 : nz], lanes[0:1])


def read_faces(refs, specs, j):
    got = {axis: [] for axis in AXES}
    for ref, (axis, r, _) in zip(refs, specs):
        got[axis].append(ref[j : j + 1, :] if axis == "gz" else ref[j])
    return got


def ghosts_of(axis, faces, like):
    zero = jnp.zeros(like, F32)
    if not faces:
        return zero, zero
    index, count = lax.axis_index(axis), lax.axis_size(axis)
    even = index % 2 == 0
    second = faces[1] if len(faces) > 1 else zero
    low = jnp.where(even, second, faces[0])
    high = jnp.where(even, faces[0], second)
    return jnp.where(index > 0, low, zero), jnp.where(index < count - 1, high, zero)


def embed_z(pair, shape):
    nx, ny, nz = shape
    low, high = pair
    return jnp.concatenate([low, jnp.zeros((nz - 2, nx * ny), F32), high], axis=0).T.reshape(shape)


def interior(t, c):
    shape = t.shape
    _, ny, nz = shape
    gain = jnp.zeros(shape, F32)
    weight = jnp.zeros(shape, F32)
    wx = 0.5 * (c[:-1] + c[1:])
    none = jnp.zeros((1, ny, nz), F32)
    w_low = jnp.concatenate([none, wx], axis=0)
    w_high = jnp.concatenate([wx, none], axis=0)
    t_low = jnp.concatenate([none, t[:-1]], axis=0)
    t_high = jnp.concatenate([t[1:], none], axis=0)
    gain = gain + w_low * t_low + w_high * t_high
    weight = weight + w_low + w_high
    for dim, n in ((1, ny), (2, nz)):
        at = iota(shape, dim)
        for shift, edge in ((1, 0), (n - 1, n - 1)):
            w = jnp.where(at == edge, 0.0, 0.5 * (c + pltpu.roll(c, shift, dim)))
            gain = gain + w * pltpu.roll(t, shift, dim)
            weight = weight + w
    return gain, weight


def shards(
    initial_hydraulic_head,
    well_discharge,
    local_facet_coupling,
    diagonal_capacity,
    crossing_permeability,
    crossing_partner_number,
    liquid_thermal_state,
    transfer_factor,
    host_voxel_number,
    stone_thermal_state,
    matrix_diffusivity,
):
    nb, links = crossing_partner_number.shape
    tri = initial_hydraulic_head.shape[1]
    shape = stone_thermal_state.shape
    nx, ny, nz = shape
    rows_n = nx * ny
    n = group_size()
    low = lax.axis_size("gy")
    pairs = by_pairs() and 4 * nb == tri
    specs2 = face_specs(shape, 2)
    specs1 = face_specs(shape, 1)
    xy = [i for i, spec in enumerate(specs2) if spec[0] != "gz"]
    zs = [i for i, spec in enumerate(specs2) if spec[0] == "gz"]
    blk = sds((nb, tri))
    slab = sds(shape)
    small = -(-2 * links // 8) * 8
    group = 8
    chunks = nb // group

    def load(copies):
        copies = [pltpu.make_async_copy(src, dst, sem) for src, dst, sem in copies]
        for copy in copies:
            copy.start()
        return copies

    def inner_of(a_ref, h, ready=None):
        h = h.astype(BF16)
        rows = []
        for b in range(0, nb, group):
            if ready:
                ready(b // group)
            both = dot(h[b : b + group, :], a_ref[b : b + group].reshape(group * tri, tri), 1, 1)
            rows += [both[i : i + 1, i * tri : (i + 1) * tri] for i in range(group)]
        return jnp.concatenate(rows, axis=0)

    def mix_of(ids, perm):
        at = iota((n * nb, ids.shape[1]), 0)
        mix = jnp.zeros(at.shape, F32)
        for k in range(links):
            mix = mix + jnp.where(at == ids[k : k + 1, :], perm[k : k + 1, :], 0.0)
        return mix

    def pre(*refs):
        hbm, (send_ref, w_ref, *rock, a_ref), (ids_ref, perm_ref, den_ref, h_ref, sems) = refs[:11], refs[11:19], refs[19:]
        a_hbm = hbm[5]
        pieces = list(zip(hbm[:5], (ids_ref, perm_ref, den_ref, h_ref, w_ref)))
        for i in range(chunks):
            part = pl.ds(i * group, group)
            pieces.append((a_hbm.at[part], a_ref.at[part]))
        pieces += list(zip(hbm[6:], rock))
        copies = load([(src, dst, sems.at[i]) for i, (src, dst) in enumerate(pieces)])
        send_ref[3 * nb :, :] = jnp.zeros((small, tri), F32)
        for copy in copies[:5]:
            copy.wait()
        perm = perm_ref[...]
        send_ref[3 * nb : 3 * nb + links, :nb] = ids_ref[...].astype(F32)
        send_ref[3 * nb + links : 3 * nb + 2 * links, :nb] = perm
        rows = jnp.concatenate([perm, jnp.zeros((-links % 8, nb), F32)], axis=0)
        send_ref[2 * nb : 3 * nb, :] = den_ref[...] + dot(rows, jnp.ones((rows.shape[0], tri), F32), 0, 0, HIGH)
        h = h_ref[...]
        send_ref[:nb, :] = h
        send_ref[nb : 2 * nb, :] = w_ref[...] + inner_of(a_ref, h, lambda i: copies[5 + i].wait())
        for copy in copies[5 + chunks :]:
            copy.wait()

    def rock(t_ref, c_ref, *faces):
        write_faces(faces, specs2, (t_ref[...], c_ref[...]))

    def both(w_ref, a_ref, *rest):
        slots, rest = rest[:n], rest[n:]
        faces, (h_ref, mix_ref, *sends) = rest[: len(xy)], rest[len(xy) :]
        me = lax.axis_index("gx") * low + lax.axis_index("gy")
        heads = jnp.concatenate([s[:nb, :] for s in slots], axis=0)
        per = tri // nb
        first = []
        for g in range(0, n, per):
            table = slots[g][3 * nb :, :]
            for i in range(1, per):
                table = table + pltpu.roll(slots[g + i][3 * nb :, :], i * nb, 1)
            ids = table[:links, :].astype(jnp.int32) ^ (me * nb)
            mix = mix_of(ids, table[links : 2 * links, :])
            if g == 0:
                mix_ref[...] = mix
            across = dot(mix, heads, 0, 0, HIGH)
            for i in range(per):
                s = slots[g + i]
                first.append((s[nb : 2 * nb, :] + across[i * nb : (i + 1) * nb, :]) / s[2 * nb : 3 * nb, :])
        inner = inner_of(a_ref, first[0])
        across = dot(mix_ref[...], jnp.concatenate(first, axis=0), 0, 0, HIGH)[:nb, :]
        h = (w_ref[...] + inner + across) / slots[0][2 * nb : 3 * nb, :]
        h_ref[...] = h
        for send, face in zip(sends, faces):
            send[:nb, :] = h
            half = face.shape[1]
            send[nb : nb + half, :] = face[0]
            send[nb + half : nb + 2 * half, :] = face[1]

    def inner_body(a_ref, h_ref, o_ref):
        o_ref[...] = inner_of(a_ref, h_ref[...])

    def sweep(w_ref, den_ref, mix_ref, inner_ref, heads):
        across = dot(mix_ref[...], heads, 0, 0, HIGH)[:nb, :]
        return (w_ref[...] + inner_ref[...] + across) / den_ref[...]

    def gather(first, t_ref, hv_ref, liq_ref, tf_ref, q_ref, hot_ref):
        t = t_ref[...].reshape(rows_n, nz)
        hi = t.astype(BF16)
        lo = (t - hi.astype(F32)).astype(BF16)
        parts = jnp.concatenate([hi, lo], axis=1)
        hv = hv_ref[...]
        step = 4
        half = hot_ref.shape[1] // tri
        for b in range(0, half, step):
            cell = jnp.concatenate([hv[first + i : first + i + 1, :] for i in range(b, b + step)], axis=1)
            width = step * tri
            mine = lax.broadcasted_iota(jnp.int16, (rows_n, width), 0) == (cell // nz).astype(jnp.int16)
            hot = jnp.where(mine, jnp.ones((), BF16), jnp.zeros((), BF16))
            hot_ref[:, b * tri : b * tri + width] = hot
            rows = dot(parts, hot, 0, 0)
            rows = rows[:nz] + rows[nz:]
            value = jnp.sum(jnp.where(iota((nz, width), 0) == cell % nz, rows, 0.0), axis=0, keepdims=True)
            for i in range(step):
                q_ref[b + i : b + i + 1, :] = value[:, i * tri : (i + 1) * tri]
        own = slice(first, first + half)
        q_ref[...] = tf_ref[own, :] * (liq_ref[own, :] - q_ref[...])

    def base(t_ref, c_ref, *rest):
        got, (u_ref, keep_ref, wz_ref) = rest[: len(zs)], rest[len(zs) :]
        specs = [specs2[i] for i in zs]
        t, c = t_ref[...], c_ref[...]
        tz = ghosts_of("gz", read_faces(got, specs, 0)["gz"], (1, rows_n))
        cz = ghosts_of("gz", read_faces(got, specs, 1)["gz"], (1, rows_n))
        gain, weight = interior(t, c)
        at = iota(shape, 2)
        wz = jnp.where((at == 0) | (at == nz - 1), 0.5 * (c + embed_z(cz, shape)), 0.0)
        keep = 1.0 - weight - wz
        wz_ref[...] = wz
        keep_ref[...] = keep
        u_ref[...] = gain + t * keep + wz * embed_z(tz, shape)

    def add_sides(u_ref, t_ref, wx_ref, wy_ref, gx, gy):
        for i, at in enumerate((0, nx - 1)):
            u_ref[at] = u_ref[at] + wx_ref[i] * (gx[i] - t_ref[at])
        for i, at in enumerate((0, ny - 1)):
            u_ref[:, at, :] = u_ref[:, at, :] + wy_ref[i] * (gy[i] - t_ref[:, at, :])

    def heat(get_sides, get_heads, ns, *refs):
        mix_ref, den_ref, w_ref, inner_ref, q1_ref, q2_ref, hv_ref, hot1_ref, hot2_ref, u_ref, t0_ref, c_ref = refs[:12]
        got, rest = refs[12 : 12 + ns], refs[12 + ns :]
        h_ref, f_ref, t_ref, wx_ref, wy_ref, *faces = rest[:-1]
        pick_ref = rest[-1]
        h = sweep(w_ref, den_ref, mix_ref, inner_ref, get_heads(got))
        h_ref[...] = h
        q = jnp.concatenate([q1_ref[...], q2_ref[...]], axis=0)
        flux = q * jnp.sqrt(1.0 + h * h)
        hi = flux.astype(BF16)
        lo = (flux - hi.astype(F32)).astype(BF16)
        lane = (hv_ref[...] % nz).astype(jnp.int16)
        at = lax.broadcasted_iota(jnp.int16, (nz, tri), 0)
        none = jnp.zeros((), BF16)
        for b in range(nb):
            mine = at == lane[b : b + 1, :]
            pick_ref[:nz, b * tri : (b + 1) * tri] = jnp.where(mine, hi[b : b + 1, :], none)
            pick_ref[nz:, b * tri : (b + 1) * tri] = jnp.where(mine, lo[b : b + 1, :], none)
        half = hot1_ref.shape[1]
        parts = dot(hot1_ref[...], pick_ref[:, :half], 1, 1) + dot(hot2_ref[...], pick_ref[:, half:], 1, 1)
        f = (parts[:, :nz] + parts[:, nz:]).reshape(shape)
        f_ref[...] = f
        t_ref[...] = u_ref[...] + f
        tx, ty = get_sides(got, 0)
        cx, cy = get_sides(got, 1)
        for i, at in enumerate((0, nx - 1)):
            wx_ref[i] = 0.5 * (c_ref[at] + cx[i])
        for i, at in enumerate((0, ny - 1)):
            wy_ref[i] = 0.5 * (c_ref[:, at, :] + cy[i])
        add_sides(t_ref, t0_ref, wx_ref, wy_ref, tx, ty)
        write_faces(faces, specs1, (t_ref[...],))

    def middle(t_ref, f_ref, c_ref, keep_ref, v_ref):
        t = t_ref[...]
        gain, _ = interior(t, c_ref[...])
        v_ref[...] = f_ref[...] + t * keep_ref[...] + gain

    def last(h_ref, v_ref, t_ref, wx_ref, wy_ref, wz_ref, *rest):
        got, (head_ref, o_ref) = rest[:-2], rest[-2:]
        head_ref[...] = h_ref[...]
        faces = read_faces(got, specs1, 0)
        o_ref[...] = v_ref[...] + wz_ref[...] * embed_z(ghosts_of("gz", faces["gz"], (1, rows_n)), shape)
        gx = ghosts_of("gx", faces["gx"], (ny, nz))
        gy = ghosts_of("gy", faces["gy"], (nx, nz))
        add_sides(o_ref, t_ref, wx_ref, wy_ref, gx, gy)

    send, w, t, c, hv, liq, tf, a = call(
        pre,
        [sds((3 * nb + small, tri)), blk, slab, slab, sds((nb, tri), jnp.int32), blk, blk]
        + [sds(local_facet_coupling.shape, BF16)],
        crossing_partner_number.T,
        crossing_permeability.T,
        diagonal_capacity,
        initial_hydraulic_head,
        well_discharge,
        local_facet_coupling,
        stone_thermal_state,
        matrix_diffusivity,
        host_voxel_number,
        liquid_thermal_state,
        transfer_factor,
        scratch=[pltpu.VMEM((links, nb), jnp.int32), pltpu.VMEM((links, nb), F32)]
        + [pltpu.VMEM((nb, tri), F32)] * 2
        + [pltpu.SemaphoreType.DMA((10 + chunks,))],
        hbm=11,
    )
    if pairs:
        slots = meet({k: send for k in range(n - 1, 0, -1) if not k & low}, send)
    faces = call(rock, [sds(s) for _, _, s in specs2], t, c)
    got_z = exchange([faces[i] for i in zs], [specs2[i] for i in zs])
    if pairs:
        y_at, xa_at, xb_at = 1, low, 2 * low
        order = {"gx": (xa_at, xb_at), "gy": (y_at,)}
        rides = [order[specs2[i][0]][specs2[i][1]] for i in xy]
        h, mix, *sends = call(
            both,
            [blk, sds((n * nb, tri))] + [sds((nb + 2 * specs2[i][2][1], tri)) for i in xy],
            w,
            a,
            send,
            *[slots[k] for k in range(1, n)],
            *[faces[i] for i in xy],
        )
        ride = dict(zip(rides, sends))
        slots = meet({k: ride.get(k, h) for k in range(n - 1, 0, -1) if not k & low}, ride[low])
        den = send[2 * nb : 3 * nb]
        got = [h] + [slots[k] for k in range(1, n)]

        def get_heads(refs):
            return jnp.concatenate([r[:nb, :] for r in refs], axis=0)

        def get_sides(refs, j):
            x_rows, y_rows = slice(nb + j * ny, nb + (j + 1) * ny), slice(nb + j * nx, nb + (j + 1) * nx)
            gx = ghosts_of("gx", [refs[xa_at][x_rows, :], refs[xb_at | low][x_rows, :]], (ny, nz))
            return gx, ghosts_of("gy", [refs[y_at][y_rows, :]], (nx, nz))
    else:
        den = send[2 * nb : 3 * nb]
        h = initial_hydraulic_head
        ids = jnp.zeros((small, tri), jnp.int32).at[:links, :nb].set(crossing_partner_number.T)
        perm = send[3 * nb + links : 3 * nb + 2 * links]

        def mix_body(ids_ref, perm_ref, mix_ref):
            mix_ref[...] = mix_of(ids_ref[...], perm_ref[...])

        def sweep_body(w_ref, den_ref, mix_ref, inner_ref, heads_ref, h_ref):
            h_ref[...] = sweep(w_ref, den_ref, mix_ref, inner_ref, heads_ref[...])

        mix = call(mix_body, sds((n * nb, tri)), ids[:links], perm)
        for _ in range(SWEEPS - 1):
            heads = lax.all_gather(h, GROUP, axis=0, tiled=True)
            inner = call(inner_body, blk, a, h)
            h = call(sweep_body, blk, w, den, mix, inner, heads)
        got = [lax.all_gather(h, GROUP, axis=0, tiled=True)]
        got += exchange([faces[i] for i in xy], [specs2[i] for i in xy])

        def get_heads(refs):
            return refs[0][...]

        def get_sides(refs, j):
            sides = read_faces(refs[1:], [specs2[i] for i in xy], j)
            return ghosts_of("gx", sides["gx"], (ny, nz)), ghosts_of("gy", sides["gy"], (nx, nz))

    inner = call(inner_body, blk, a, h)
    half = nb // 2
    parts = [
        call(functools.partial(gather, i * half), (sds((half, tri)), sds((rows_n, half * tri), BF16)), t, hv, liq, tf)
        for i in range(2)
    ]
    (q1, hot1), (q2, hot2) = parts
    u, keep, wz = call(base, (slab, slab, slab), t, c, *got_z)
    h, f, t1, wx, wy, *faces = call(
        functools.partial(heat, get_sides, get_heads, len(got)),
        [blk, slab, slab, sds((2, ny, nz)), sds((2, nx, nz))] + [sds(s) for _, _, s in specs1],
        mix,
        den,
        w,
        inner,
        q1,
        q2,
        hv,
        hot1,
        hot2,
        u,
        t,
        c,
        *got,
        scratch=[pltpu.VMEM((2 * nz, nb * tri), BF16)],
    )
    got = exchange(faces, specs1)
    v = call(middle, slab, t1, f, c, keep)
    h, out = call(last, (blk, slab), h, v, t1, wx, wy, wz, *got)
    return (h, out)


def solution(mesh):
    block = P(AXES, None)
    rock = P(*AXES)
    in_specs = (block, block, P(AXES, None, None)) + (block,) * 6 + (rock, rock)

    return jax.shard_map(shards, mesh=mesh, in_specs=in_specs, out_specs=(block, rock), check_vma=False)
```

```python
import functools
import itertools

import jax
import jax.numpy as jnp
from jax import lax
from jax.experimental import pallas as pl
from jax.experimental.pallas import tpu as pltpu
from jax.sharding import PartitionSpec as P


SWEEPS = 3
AXES = ("gx", "gy", "gz")
GROUP = ("gx", "gy")
F32 = jnp.float32
BF16 = jnp.bfloat16
HIGH = lax.Precision.HIGHEST


def call(body, out_shape, *args, scratch=(), hbm=0):
    vmem = pl.BlockSpec(memory_space=pltpu.VMEM)
    args = [pltpu.with_memory_space_constraint(x, pltpu.HBM) for x in args[:hbm]] + list(args[hbm:])
    return pl.pallas_call(
        body,
        out_shape=out_shape,
        in_specs=[pl.BlockSpec(memory_space=pltpu.HBM)] * hbm + [vmem] * (len(args) - hbm),
        scratch_shapes=scratch,
        compiler_params=pltpu.CompilerParams(vmem_limit_bytes=48 << 20),
    )(*args)


def sds(shape, dtype=F32):
    return jax.ShapeDtypeStruct(shape, dtype)


def iota(shape, dim):
    return lax.broadcasted_iota(jnp.int32, shape, dim)


def dot(a, b, ca, cb, precision=None):
    return lax.dot_general(
        a, b, (((ca,), (cb,)), ((), ())), precision=precision, preferred_element_type=F32
    )


def split(x):
    hi = x.astype(BF16)
    return hi, (x - hi.astype(F32)).astype(BF16)


def dot3(a, b, ca, cb):
    return dot(a[0], b[0], ca, cb) + (dot(a[0], b[1], ca, cb) + dot(a[1], b[0], ca, cb))


def group_size():
    return lax.axis_size("gx") * lax.axis_size("gy")


def by_pairs():
    return lax.axis_size("gx") == 4 and lax.axis_size("gy") == 2


def swap(x, k):
    n = group_size()
    return lax.ppermute(x, GROUP, [(i, i ^ k) for i in range(n)])


def meet(direct, own):
    low = lax.axis_size("gy")
    slots = {k: swap(x, k) for k, x in direct.items()}
    slots[low] = swap(own, low)
    for k in direct:
        slots[k | low] = swap(slots[k], low)
    return slots


def partner(axis, r, where):
    at, count, other = where[axis], lax.axis_size(axis), dict(where)
    up = at % 2 == r
    to = at + 1 if up else at - 1
    if 0 <= to < count:
        other[axis] = to
    elif axis == "gx":
        other[axis] = at if count % 2 else count - 1 - at
    elif lax.axis_size("gx") % 2 == 0:
        other["gx"] = where["gx"] ^ 1
    return other


def swap_list(axis, r):
    sizes = [lax.axis_size(a) for a in AXES]
    pairs = []
    for i, at in enumerate(itertools.product(*map(range, sizes))):
        other = partner(axis, r, dict(zip(AXES, at)))
        j = 0
        for a, size in zip(AXES, sizes):
            j = j * size + other[a]
        pairs.append((i, j))
    return pairs


def rounds_of(axis):
    count = lax.axis_size(axis)
    return 0 if count == 1 else 1 if count == 2 else 2


def face_specs(shape, lead):
    nx, ny, nz = shape
    full = {"gx": (lead, ny, nz), "gy": (lead, nx, nz), "gz": (lead, nx * ny)}
    return [(axis, r, full[axis]) for axis in AXES for r in range(rounds_of(axis))]


def exchange(faces, specs):
    out = []
    for face, (axis, r, _) in zip(faces, specs):
        out.append(lax.ppermute(face, AXES, swap_list(axis, r)))
    return out


def write_faces(refs, specs, fields):
    for j, t in enumerate(fields):
        nx, ny, nz = t.shape
        lanes = t.reshape(nx * ny, nz).T
        for ref, (axis, r, _) in zip(refs, specs):
            even = lax.axis_index(axis) % 2 == 0
            high = even if r == 0 else jnp.logical_not(even)
            if axis == "gx":
                ref[j] = jnp.where(high, t[nx - 1], t[0])
            elif axis == "gy":
                ref[j] = jnp.where(high, t[:, ny - 1, :], t[:, 0, :])
            else:
                ref[j : j + 1, :] = jnp.where(high, lanes[nz - 1 : nz], lanes[0:1])


def read_faces(refs, specs, j):
    got = {axis: [] for axis in AXES}
    for ref, (axis, r, _) in zip(refs, specs):
        got[axis].append(ref[j : j + 1, :] if axis == "gz" else ref[j])
    return got


def ghosts_of(axis, faces, like):
    zero = jnp.zeros(like, F32)
    if not faces:
        return zero, zero
    index, count = lax.axis_index(axis), lax.axis_size(axis)
    even = index % 2 == 0
    second = faces[1] if len(faces) > 1 else zero
    low = jnp.where(even, second, faces[0])
    high = jnp.where(even, faces[0], second)
    return jnp.where(index > 0, low, zero), jnp.where(index < count - 1, high, zero)


def embed_z(pair, shape):
    nx, ny, nz = shape
    low, high = pair
    return jnp.concatenate([low, jnp.zeros((nz - 2, nx * ny), F32), high], axis=0).T.reshape(shape)


def interior(t, c):
    shape = t.shape
    _, ny, nz = shape
    gain = jnp.zeros(shape, F32)
    weight = jnp.zeros(shape, F32)
    wx = 0.5 * (c[:-1] + c[1:])
    none = jnp.zeros((1, ny, nz), F32)
    w_low = jnp.concatenate([none, wx], axis=0)
    w_high = jnp.concatenate([wx, none], axis=0)
    t_low = jnp.concatenate([none, t[:-1]], axis=0)
    t_high = jnp.concatenate([t[1:], none], axis=0)
    gain = gain + w_low * t_low + w_high * t_high
    weight = weight + w_low + w_high
    for dim, n in ((1, ny), (2, nz)):
        at = iota(shape, dim)
        for shift, edge in ((1, 0), (n - 1, n - 1)):
            w = jnp.where(at == edge, 0.0, 0.5 * (c + pltpu.roll(c, shift, dim)))
            gain = gain + w * pltpu.roll(t, shift, dim)
            weight = weight + w
    return gain, weight


def shards(
    initial_hydraulic_head,
    well_discharge,
    local_facet_coupling,
    diagonal_capacity,
    crossing_permeability,
    crossing_partner_number,
    liquid_thermal_state,
    transfer_factor,
    host_voxel_number,
    stone_thermal_state,
    matrix_diffusivity,
):
    nb, links = crossing_partner_number.shape
    tri = initial_hydraulic_head.shape[1]
    shape = stone_thermal_state.shape
    nx, ny, nz = shape
    rows_n = nx * ny
    n = group_size()
    low = lax.axis_size("gy")
    pairs = by_pairs() and 4 * nb == tri
    specs2 = face_specs(shape, 2)
    specs1 = face_specs(shape, 1)
    xy = [i for i, spec in enumerate(specs2) if spec[0] != "gz"]
    zs = [i for i, spec in enumerate(specs2) if spec[0] == "gz"]
    blk = sds((nb, tri))
    slab = sds(shape)
    small = -(-2 * links // 8) * 8
    group = 8
    chunks = nb // group

    def load(copies):
        copies = [pltpu.make_async_copy(src, dst, sem) for src, dst, sem in copies]
        for copy in copies:
            copy.start()
        return copies

    def inner_of(a_ref, h, ready=None):
        h = h.astype(BF16)
        rows = []
        for b in range(0, nb, group):
            if ready:
                ready(b // group)
            both = dot(h[b : b + group, :], a_ref[b : b + group].reshape(group * tri, tri), 1, 1)
            rows += [both[i : i + 1, i * tri : (i + 1) * tri] for i in range(group)]
        return jnp.concatenate(rows, axis=0)

    def mix_of(ids, perm):
        at = iota((n * nb, ids.shape[1]), 0)
        mix = jnp.zeros(at.shape, F32)
        for k in range(links):
            mix = mix + jnp.where(at == ids[k : k + 1, :], perm[k : k + 1, :], 0.0)
        return mix

    def pre(*refs):
        hbm, (send_ref, w_ref, *rock, a_ref), (ids_ref, perm_ref, den_ref, h_ref, sems) = refs[:11], refs[11:19], refs[19:]
        a_hbm = hbm[5]
        pieces = list(zip(hbm[:5], (ids_ref, perm_ref, den_ref, h_ref, w_ref)))
        for i in range(chunks):
            part = pl.ds(i * group, group)
            pieces.append((a_hbm.at[part], a_ref.at[part]))
        pieces += list(zip(hbm[6:], rock))
        copies = load([(src, dst, sems.at[i]) for i, (src, dst) in enumerate(pieces)])
        send_ref[3 * nb :, :] = jnp.zeros((small, tri), F32)
        for copy in copies[:5]:
            copy.wait()
        perm = perm_ref[...]
        send_ref[3 * nb : 3 * nb + links, :nb] = ids_ref[...].astype(F32)
        send_ref[3 * nb + links : 3 * nb + 2 * links, :nb] = perm
        rows = jnp.concatenate([perm, jnp.zeros((-links % 8, nb), F32)], axis=0)
        send_ref[2 * nb : 3 * nb, :] = den_ref[...] + dot(rows, jnp.ones((rows.shape[0], tri), F32), 0, 0, HIGH)
        h = h_ref[...]
        send_ref[:nb, :] = h
        send_ref[nb : 2 * nb, :] = w_ref[...] + inner_of(a_ref, h, lambda i: copies[5 + i].wait())
        for copy in copies[5 + chunks :]:
            copy.wait()

    def own_mix(table, mix_ref):
        ids = table[:links, :].astype(jnp.int32)
        if pairs:
            ids = ids ^ ((lax.axis_index("gx") * low + lax.axis_index("gy")) * nb)
        mix = split(mix_of(ids, table[links : 2 * links, :]).T[:nb, :])
        mix_ref[0], mix_ref[1] = mix

    def rock(t_ref, c_ref, send_ref, *outs):
        write_faces(outs[1:], specs2, (t_ref[...], c_ref[...]))
        own_mix(send_ref[3 * nb :, :], outs[0])

    def both(w_ref, a_ref, mix_ref, *rest):
        slots, rest = rest[:n], rest[n:]
        faces, (h_ref, *sends) = rest[: len(xy)], rest[len(xy) :]
        me = lax.axis_index("gx") * low + lax.axis_index("gy")
        heads = split(jnp.concatenate([s[:nb, :] for s in slots], axis=0))
        per = tri // nb
        tables = []
        for g in range(0, n, per):
            table = slots[g][3 * nb :, :]
            for i in range(1, per):
                table = table + pltpu.roll(slots[g + i][3 * nb :, :], i * nb, 1)
            tables.append(table)
        table = jnp.concatenate(tables, axis=1)
        ids = table[:links, :].astype(jnp.int32) ^ (me * nb)
        across = dot3(split(mix_of(ids, table[links : 2 * links, :])), heads, 0, 0)
        first = []
        for k, s in enumerate(slots):
            first.append((s[nb : 2 * nb, :] + across[k * nb : (k + 1) * nb, :]) / s[2 * nb : 3 * nb, :])
        inner = inner_of(a_ref, first[0])
        across = dot3(mix_ref, split(jnp.concatenate(first, axis=0)), 1, 0)
        h = (w_ref[...] + inner + across) / slots[0][2 * nb : 3 * nb, :]
        h_ref[...] = h
        for send, face in zip(sends, faces):
            send[:nb, :] = h
            half = face.shape[1]
            send[nb : nb + half, :] = face[0]
            send[nb + half : nb + 2 * half, :] = face[1]

    def inner_body(a_ref, h_ref, o_ref):
        o_ref[...] = inner_of(a_ref, h_ref[...])

    def sweep(w_ref, den_ref, mix_ref, inner_ref, heads):
        across = dot3(mix_ref, split(heads), 1, 0)
        return (w_ref[...] + inner_ref[...] + across) / den_ref[...]

    def gather(first, t_ref, hv_ref, liq_ref, tf_ref, q_ref, hot_ref):
        t = t_ref[...].reshape(rows_n, nz)
        hi = t.astype(BF16)
        lo = (t - hi.astype(F32)).astype(BF16)
        parts = jnp.concatenate([hi, lo], axis=1)
        hv = hv_ref[...]
        step = 4
        half = hot_ref.shape[1] // tri
        for b in range(0, half, step):
            cell = jnp.concatenate([hv[first + i : first + i + 1, :] for i in range(b, b + step)], axis=1)
            width = step * tri
            mine = lax.broadcasted_iota(jnp.int16, (rows_n, width), 0) == (cell // nz).astype(jnp.int16)
            hot = jnp.where(mine, jnp.ones((), BF16), jnp.zeros((), BF16))
            hot_ref[:, b * tri : b * tri + width] = hot
            rows = dot(parts, hot, 0, 0)
            rows = rows[:nz] + rows[nz:]
            value = jnp.sum(jnp.where(iota((nz, width), 0) == cell % nz, rows, 0.0), axis=0, keepdims=True)
            for i in range(step):
                q_ref[b + i : b + i + 1, :] = value[:, i * tri : (i + 1) * tri]
        own = slice(first, first + half)
        q_ref[...] = tf_ref[own, :] * (liq_ref[own, :] - q_ref[...])

    def base(t_ref, c_ref, *rest):
        got, (u_ref, keep_ref, wz_ref) = rest[: len(zs)], rest[len(zs) :]
        specs = [specs2[i] for i in zs]
        t, c = t_ref[...], c_ref[...]
        tz = ghosts_of("gz", read_faces(got, specs, 0)["gz"], (1, rows_n))
        cz = ghosts_of("gz", read_faces(got, specs, 1)["gz"], (1, rows_n))
        gain, weight = interior(t, c)
        at = iota(shape, 2)
        wz = jnp.where((at == 0) | (at == nz - 1), 0.5 * (c + embed_z(cz, shape)), 0.0)
        keep = 1.0 - weight - wz
        wz_ref[...] = wz
        keep_ref[...] = keep
        u_ref[...] = gain + t * keep + wz * embed_z(tz, shape)

    def add_sides(u_ref, t_ref, wx_ref, wy_ref, gx, gy):
        for i, at in enumerate((0, nx - 1)):
            u_ref[at] = u_ref[at] + wx_ref[i] * (gx[i] - t_ref[at])
        for i, at in enumerate((0, ny - 1)):
            u_ref[:, at, :] = u_ref[:, at, :] + wy_ref[i] * (gy[i] - t_ref[:, at, :])

    def heat(get_sides, get_heads, ns, *refs):
        mix_ref, den_ref, w_ref, inner_ref, q1_ref, q2_ref, hv_ref, hot1_ref, hot2_ref, u_ref, t0_ref, c_ref = refs[:12]
        got, rest = refs[12 : 12 + ns], refs[12 + ns :]
        h_ref, f_ref, t_ref, wx_ref, wy_ref, *faces = rest[:-1]
        pick_ref = rest[-1]
        h = sweep(w_ref, den_ref, mix_ref, inner_ref, get_heads(got))
        h_ref[...] = h
        q = jnp.concatenate([q1_ref[...], q2_ref[...]], axis=0)
        flux = q * jnp.sqrt(1.0 + h * h)
        hi = flux.astype(BF16)
        lo = (flux - hi.astype(F32)).astype(BF16)
        lane = (hv_ref[...] % nz).astype(jnp.int16)
        at = lax.broadcasted_iota(jnp.int16, (nz, tri), 0)
        none = jnp.zeros((), BF16)
        for b in range(nb):
            mine = at == lane[b : b + 1, :]
            pick_ref[:nz, b * tri : (b + 1) * tri] = jnp.where(mine, hi[b : b + 1, :], none)
            pick_ref[nz:, b * tri : (b + 1) * tri] = jnp.where(mine, lo[b : b + 1, :], none)
        half = hot1_ref.shape[1]
        parts = dot(hot1_ref[...], pick_ref[:, :half], 1, 1) + dot(hot2_ref[...], pick_ref[:, half:], 1, 1)
        f = (parts[:, :nz] + parts[:, nz:]).reshape(shape)
        f_ref[...] = f
        t_ref[...] = u_ref[...] + f
        tx, ty = get_sides(got, 0)
        cx, cy = get_sides(got, 1)
        for i, at in enumerate((0, nx - 1)):
            wx_ref[i] = 0.5 * (c_ref[at] + cx[i])
        for i, at in enumerate((0, ny - 1)):
            wy_ref[i] = 0.5 * (c_ref[:, at, :] + cy[i])
        add_sides(t_ref, t0_ref, wx_ref, wy_ref, tx, ty)
        write_faces(faces, specs1, (t_ref[...],))

    def middle(t_ref, f_ref, c_ref, keep_ref, v_ref):
        t = t_ref[...]
        gain, _ = interior(t, c_ref[...])
        v_ref[...] = f_ref[...] + t * keep_ref[...] + gain

    def last(h_ref, v_ref, t_ref, wx_ref, wy_ref, wz_ref, *rest):
        got, (head_ref, o_ref) = rest[:-2], rest[-2:]
        head_ref[...] = h_ref[...]
        faces = read_faces(got, specs1, 0)
        o_ref[...] = v_ref[...] + wz_ref[...] * embed_z(ghosts_of("gz", faces["gz"], (1, rows_n)), shape)
        gx = ghosts_of("gx", faces["gx"], (ny, nz))
        gy = ghosts_of("gy", faces["gy"], (nx, nz))
        add_sides(o_ref, t_ref, wx_ref, wy_ref, gx, gy)

    send, w, t, c, hv, liq, tf, a = call(
        pre,
        [sds((3 * nb + small, tri)), blk, slab, slab, sds((nb, tri), jnp.int32), blk, blk]
        + [sds(local_facet_coupling.shape, BF16)],
        crossing_partner_number.T,
        crossing_permeability.T,
        diagonal_capacity,
        initial_hydraulic_head,
        well_discharge,
        local_facet_coupling,
        stone_thermal_state,
        matrix_diffusivity,
        host_voxel_number,
        liquid_thermal_state,
        transfer_factor,
        scratch=[pltpu.VMEM((links, nb), jnp.int32), pltpu.VMEM((links, nb), F32)]
        + [pltpu.VMEM((nb, tri), F32)] * 2
        + [pltpu.SemaphoreType.DMA((10 + chunks,))],
        hbm=11,
    )
    if pairs:
        slots = meet({k: send for k in range(n - 1, 0, -1) if not k & low}, send)
    mix, *faces = call(rock, [sds((2, nb, n * nb), BF16)] + [sds(s) for _, _, s in specs2], t, c, send)
    got_z = exchange([faces[i] for i in zs], [specs2[i] for i in zs])
    if pairs:
        y_at, xa_at, xb_at = 1, low, 2 * low
        order = {"gx": (xa_at, xb_at), "gy": (y_at,)}
        rides = [order[specs2[i][0]][specs2[i][1]] for i in xy]
        h, *sends = call(
            both,
            [blk] + [sds((nb + 2 * specs2[i][2][1], tri)) for i in xy],
            w,
            a,
            mix,
            send,
            *[slots[k] for k in range(1, n)],
            *[faces[i] for i in xy],
        )
        ride = dict(zip(rides, sends))
        slots = meet({k: ride.get(k, h) for k in range(n - 1, 0, -1) if not k & low}, ride[low])
        den = send[2 * nb : 3 * nb]
        got = [h] + [slots[k] for k in range(1, n)]

        def get_heads(refs):
            return jnp.concatenate([r[:nb, :] for r in refs], axis=0)

        def get_sides(refs, j):
            x_rows, y_rows = slice(nb + j * ny, nb + (j + 1) * ny), slice(nb + j * nx, nb + (j + 1) * nx)
            gx = ghosts_of("gx", [refs[xa_at][x_rows, :], refs[xb_at | low][x_rows, :]], (ny, nz))
            return gx, ghosts_of("gy", [refs[y_at][y_rows, :]], (nx, nz))
    else:
        den = send[2 * nb : 3 * nb]
        h = initial_hydraulic_head

        def sweep_body(w_ref, den_ref, mix_ref, inner_ref, heads_ref, h_ref):
            h_ref[...] = sweep(w_ref, den_ref, mix_ref, inner_ref, heads_ref[...])

        for _ in range(SWEEPS - 1):
            heads = lax.all_gather(h, GROUP, axis=0, tiled=True)
            inner = call(inner_body, blk, a, h)
            h = call(sweep_body, blk, w, den, mix, inner, heads)
        got = [lax.all_gather(h, GROUP, axis=0, tiled=True)]
        got += exchange([faces[i] for i in xy], [specs2[i] for i in xy])

        def get_heads(refs):
            return refs[0][...]

        def get_sides(refs, j):
            sides = read_faces(refs[1:], [specs2[i] for i in xy], j)
            return ghosts_of("gx", sides["gx"], (ny, nz)), ghosts_of("gy", sides["gy"], (nx, nz))

    inner = call(inner_body, blk, a, h)
    half = nb // 2
    parts = [
        call(functools.partial(gather, i * half), (sds((half, tri)), sds((rows_n, half * tri), BF16)), t, hv, liq, tf)
        for i in range(2)
    ]
    (q1, hot1), (q2, hot2) = parts
    u, keep, wz = call(base, (slab, slab, slab), t, c, *got_z)
    h, f, t1, wx, wy, *faces = call(
        functools.partial(heat, get_sides, get_heads, len(got)),
        [blk, slab, slab, sds((2, ny, nz)), sds((2, nx, nz))] + [sds(s) for _, _, s in specs1],
        mix,
        den,
        w,
        inner,
        q1,
        q2,
        hv,
        hot1,
        hot2,
        u,
        t,
        c,
        *got,
        scratch=[pltpu.VMEM((2 * nz, nb * tri), BF16)],
    )
    got = exchange(faces, specs1)
    v = call(middle, slab, t1, f, c, keep)
    h, out = call(last, (blk, slab), h, v, t1, wx, wy, wz, *got)
    return (h, out)


def solution(mesh):
    block = P(AXES, None)
    rock = P(*AXES)
    in_specs = (block, block, P(AXES, None, None)) + (block,) * 6 + (rock, rock)

    return jax.shard_map(shards, mesh=mesh, in_specs=in_specs, out_specs=(block, rock), check_vma=False)
```

```python
import functools
import itertools

import jax
import jax.numpy as jnp
from jax import lax
from jax.experimental import pallas as pl
from jax.experimental.pallas import tpu as pltpu
from jax.sharding import PartitionSpec as P


SWEEPS = 3
AXES = ("gx", "gy", "gz")
GROUP = ("gx", "gy")
F32 = jnp.float32
BF16 = jnp.bfloat16
HIGH = lax.Precision.HIGHEST


def call(body, out_shape, *args, scratch=(), hbm=0, hbm_out=False):
    vmem = pl.BlockSpec(memory_space=pltpu.VMEM)
    args = [pltpu.with_memory_space_constraint(x, pltpu.HBM) for x in args[:hbm]] + list(args[hbm:])
    return pl.pallas_call(
        body,
        out_shape=out_shape,
        in_specs=[pl.BlockSpec(memory_space=pltpu.HBM)] * hbm + [vmem] * (len(args) - hbm),
        scratch_shapes=scratch,
        **({"out_specs": jax.tree.map(lambda _: pl.BlockSpec(memory_space=pltpu.HBM), out_shape)} if hbm_out else {}),
        compiler_params=pltpu.CompilerParams(vmem_limit_bytes=48 << 20),
    )(*args)


def sds(shape, dtype=F32):
    return jax.ShapeDtypeStruct(shape, dtype)


def iota(shape, dim):
    return lax.broadcasted_iota(jnp.int32, shape, dim)


def dot(a, b, ca, cb, precision=None):
    return lax.dot_general(
        a, b, (((ca,), (cb,)), ((), ())), precision=precision, preferred_element_type=F32
    )


def split(x):
    hi = x.astype(BF16)
    return hi, (x - hi.astype(F32)).astype(BF16)


def dot3(a, b, ca, cb):
    return dot(a[0], b[0], ca, cb) + (dot(a[0], b[1], ca, cb) + dot(a[1], b[0], ca, cb))


def group_size():
    return lax.axis_size("gx") * lax.axis_size("gy")


def by_pairs():
    return lax.axis_size("gx") == 4 and lax.axis_size("gy") == 2


def swap(x, k):
    n = group_size()
    return lax.ppermute(x, GROUP, [(i, i ^ k) for i in range(n)])


def meet(direct, own):
    low = lax.axis_size("gy")
    slots = {k: swap(x, k) for k, x in direct.items()}
    slots[low] = swap(own, low)
    for k in direct:
        if k | low not in direct:
            slots[k | low] = swap(slots[k], low)
    return slots


def partner(axis, r, where):
    at, count, other = where[axis], lax.axis_size(axis), dict(where)
    up = at % 2 == r
    to = at + 1 if up else at - 1
    if 0 <= to < count:
        other[axis] = to
    elif axis == "gx":
        other[axis] = at if count % 2 else count - 1 - at
    elif lax.axis_size("gx") % 2 == 0:
        other["gx"] = where["gx"] ^ 1
    return other


def swap_list(axis, r):
    sizes = [lax.axis_size(a) for a in AXES]
    pairs = []
    for i, at in enumerate(itertools.product(*map(range, sizes))):
        other = partner(axis, r, dict(zip(AXES, at)))
        j = 0
        for a, size in zip(AXES, sizes):
            j = j * size + other[a]
        pairs.append((i, j))
    return pairs


def rounds_of(axis):
    count = lax.axis_size(axis)
    return 0 if count == 1 else 1 if count == 2 else 2


def face_specs(shape, lead):
    nx, ny, nz = shape
    full = {"gx": (lead, ny, nz), "gy": (lead, nx, nz), "gz": (lead, nx * ny)}
    return [(axis, r, full[axis]) for axis in AXES for r in range(rounds_of(axis))]


def exchange(faces, specs):
    out = []
    for face, (axis, r, _) in zip(faces, specs):
        out.append(lax.ppermute(face, AXES, swap_list(axis, r)))
    return out


def write_faces(refs, specs, fields):
    for j, t in enumerate(fields):
        nx, ny, nz = t.shape
        lanes = t.reshape(nx * ny, nz).T
        for ref, (axis, r, _) in zip(refs, specs):
            even = lax.axis_index(axis) % 2 == 0
            high = even if r == 0 else jnp.logical_not(even)
            if axis == "gx":
                ref[j] = jnp.where(high, t[nx - 1], t[0])
            elif axis == "gy":
                ref[j] = jnp.where(high, t[:, ny - 1, :], t[:, 0, :])
            else:
                ref[j : j + 1, :] = jnp.where(high, lanes[nz - 1 : nz], lanes[0:1])


def read_faces(refs, specs, j):
    got = {axis: [] for axis in AXES}
    for ref, (axis, r, _) in zip(refs, specs):
        got[axis].append(ref[j : j + 1, :] if axis == "gz" else ref[j])
    return got


def ghosts_of(axis, faces, like):
    zero = jnp.zeros(like, F32)
    if not faces:
        return zero, zero
    index, count = lax.axis_index(axis), lax.axis_size(axis)
    even = index % 2 == 0
    second = faces[1] if len(faces) > 1 else zero
    low = jnp.where(even, second, faces[0])
    high = jnp.where(even, faces[0], second)
    return jnp.where(index > 0, low, zero), jnp.where(index < count - 1, high, zero)


def embed_z(pair, shape):
    nx, ny, nz = shape
    low, high = pair
    return jnp.concatenate([low, jnp.zeros((nz - 2, nx * ny), F32), high], axis=0).T.reshape(shape)


def interior(t, c):
    shape = t.shape
    _, ny, nz = shape
    gain = jnp.zeros(shape, F32)
    weight = jnp.zeros(shape, F32)
    wx = 0.5 * (c[:-1] + c[1:])
    none = jnp.zeros((1, ny, nz), F32)
    w_low = jnp.concatenate([none, wx], axis=0)
    w_high = jnp.concatenate([wx, none], axis=0)
    t_low = jnp.concatenate([none, t[:-1]], axis=0)
    t_high = jnp.concatenate([t[1:], none], axis=0)
    gain = gain + w_low * t_low + w_high * t_high
    weight = weight + w_low + w_high
    for dim, n in ((1, ny), (2, nz)):
        at = iota(shape, dim)
        for shift, edge in ((1, 0), (n - 1, n - 1)):
            w = jnp.where(at == edge, 0.0, 0.5 * (c + pltpu.roll(c, shift, dim)))
            gain = gain + w * pltpu.roll(t, shift, dim)
            weight = weight + w
    return gain, weight


def shards(
    initial_hydraulic_head,
    well_discharge,
    local_facet_coupling,
    diagonal_capacity,
    crossing_permeability,
    crossing_partner_number,
    liquid_thermal_state,
    transfer_factor,
    host_voxel_number,
    stone_thermal_state,
    matrix_diffusivity,
):
    nb, links = crossing_partner_number.shape
    tri = initial_hydraulic_head.shape[1]
    shape = stone_thermal_state.shape
    nx, ny, nz = shape
    rows_n = nx * ny
    n = group_size()
    low = lax.axis_size("gy")
    pairs = by_pairs() and 4 * nb == tri
    specs2 = face_specs(shape, 2)
    specs1 = face_specs(shape, 1)
    xy = [i for i, spec in enumerate(specs2) if spec[0] != "gz"]
    zs = [i for i, spec in enumerate(specs2) if spec[0] == "gz"]
    blk = sds((nb, tri))
    slab = sds(shape)
    small = -(-2 * links // 8) * 8
    group = 8
    chunks = nb // group

    def load(copies):
        copies = [pltpu.make_async_copy(src, dst, sem) for src, dst, sem in copies]
        for copy in copies:
            copy.start()
        return copies

    def inner_of(a_ref, h):
        h = h.astype(BF16)
        rows = []
        for b in range(0, nb, group):
            both = dot(h[b : b + group, :], a_ref[b : b + group].reshape(group * tri, tri), 1, 1)
            rows += [both[i : i + 1, i * tri : (i + 1) * tri] for i in range(group)]
        return jnp.concatenate(rows, axis=0)

    def mix_of(ids, perm):
        at = iota((n * nb, ids.shape[1]), 0)
        mix = jnp.zeros(at.shape, F32)
        for k in range(links):
            mix = mix + jnp.where(at == ids[k : k + 1, :], perm[k : k + 1, :], 0.0)
        return mix

    def pre(*refs):
        hbm, (send_ref, w_ref, *rock, a_ref), (ids_ref, perm_ref, den_ref, h_ref, sems) = refs[:11], refs[11:19], refs[19:]
        a_hbm = hbm[5]
        pieces = list(zip(hbm[:5], (ids_ref, perm_ref, den_ref, h_ref, w_ref)))
        for i in range(chunks):
            part = pl.ds(i * group, group)
            pieces.append((a_hbm.at[part], a_ref.at[part]))
        pieces += list(zip(hbm[6:], rock))
        copies = load([(src, dst, sems.at[i]) for i, (src, dst) in enumerate(pieces)])
        send_ref[3 * nb :, :] = jnp.zeros((small, tri), F32)
        for copy in copies[: 5 + chunks]:
            copy.wait()
        perm = perm_ref[...]
        send_ref[3 * nb : 3 * nb + links, :nb] = ids_ref[...].astype(F32)
        send_ref[3 * nb + links : 3 * nb + 2 * links, :nb] = perm
        rows = jnp.concatenate([perm, jnp.zeros((-links % 8, nb), F32)], axis=0)
        send_ref[2 * nb : 3 * nb, :] = den_ref[...] + dot(rows, jnp.ones((rows.shape[0], tri), F32), 0, 0, HIGH)
        h = h_ref[...]
        send_ref[:nb, :] = h
        send_ref[nb : 2 * nb, :] = w_ref[...] + inner_of(a_ref, h)
        for copy in copies[5 + chunks :]:
            copy.wait()

    def own_mix(table, mix_ref):
        ids = table[:links, :].astype(jnp.int32)
        if pairs:
            ids = ids ^ ((lax.axis_index("gx") * low + lax.axis_index("gy")) * nb)
        mix = split(mix_of(ids, table[links : 2 * links, :]).T[:nb, :])
        mix_ref[0], mix_ref[1] = mix

    def rock(t_ref, c_ref, send_ref, *outs):
        write_faces(outs[1:], specs2, (t_ref[...], c_ref[...]))
        own_mix(send_ref[3 * nb :, :], outs[0])

    def both(w_ref, a_ref, mix_ref, *rest):
        slots, rest = rest[:n], rest[n:]
        faces, (h_ref, *sends) = rest[: len(xy)], rest[len(xy) :]
        me = lax.axis_index("gx") * low + lax.axis_index("gy")
        heads = split(jnp.concatenate([s[:nb, :] for s in slots], axis=0))
        per = tri // nb
        tables = []
        for g in range(0, n, per):
            table = slots[g][3 * nb :, :]
            for i in range(1, per):
                table = table + pltpu.roll(slots[g + i][3 * nb :, :], i * nb, 1)
            tables.append(table)
        table = jnp.concatenate(tables, axis=1)
        ids = table[:links, :].astype(jnp.int32) ^ (me * nb)
        across = dot3(split(mix_of(ids, table[links : 2 * links, :])), heads, 0, 0)
        first = []
        for k, s in enumerate(slots):
            first.append((s[nb : 2 * nb, :] + across[k * nb : (k + 1) * nb, :]) / s[2 * nb : 3 * nb, :])
        inner = inner_of(a_ref, first[0])
        across = dot3(mix_ref, split(jnp.concatenate(first, axis=0)), 1, 0)
        h = (w_ref[...] + inner + across) / slots[0][2 * nb : 3 * nb, :]
        h_ref[...] = h
        for send, face in zip(sends, faces):
            send[:nb, :] = h
            half = face.shape[1]
            send[nb : nb + half, :] = face[0]
            send[nb + half : nb + 2 * half, :] = face[1]

    def inner_body(a_ref, h_ref, o_ref):
        o_ref[...] = inner_of(a_ref, h_ref[...])

    def sweep(w_ref, den_ref, mix_ref, inner_ref, heads):
        across = dot3(mix_ref, split(heads), 1, 0)
        return (w_ref[...] + inner_ref[...] + across) / den_ref[...]

    def gather(first, t_ref, hv_ref, liq_ref, tf_ref, q_ref, hot_ref):
        t = t_ref[...].reshape(rows_n, nz)
        hi = t.astype(BF16)
        lo = (t - hi.astype(F32)).astype(BF16)
        parts = jnp.concatenate([hi, lo], axis=1)
        hv = hv_ref[...]
        step = 4
        half = hot_ref.shape[1] // tri
        for b in range(0, half, step):
            cell = jnp.concatenate([hv[first + i : first + i + 1, :] for i in range(b, b + step)], axis=1)
            width = step * tri
            mine = lax.broadcasted_iota(jnp.int16, (rows_n, width), 0) == (cell // nz).astype(jnp.int16)
            hot = jnp.where(mine, jnp.ones((), BF16), jnp.zeros((), BF16))
            hot_ref[:, b * tri : b * tri + width] = hot
            rows = dot(parts, hot, 0, 0)
            rows = rows[:nz] + rows[nz:]
            value = jnp.sum(jnp.where(iota((nz, width), 0) == cell % nz, rows, 0.0), axis=0, keepdims=True)
            for i in range(step):
                q_ref[b + i : b + i + 1, :] = value[:, i * tri : (i + 1) * tri]
        own = slice(first, first + half)
        q_ref[...] = tf_ref[own, :] * (liq_ref[own, :] - q_ref[...])

    def base(t_ref, c_ref, *rest):
        got, (u_ref, keep_ref, wz_ref) = rest[: len(zs)], rest[len(zs) :]
        specs = [specs2[i] for i in zs]
        t, c = t_ref[...], c_ref[...]
        tz = ghosts_of("gz", read_faces(got, specs, 0)["gz"], (1, rows_n))
        cz = ghosts_of("gz", read_faces(got, specs, 1)["gz"], (1, rows_n))
        gain, weight = interior(t, c)
        at = iota(shape, 2)
        wz = jnp.where((at == 0) | (at == nz - 1), 0.5 * (c + embed_z(cz, shape)), 0.0)
        keep = 1.0 - weight - wz
        wz_ref[...] = wz
        keep_ref[...] = keep
        u_ref[...] = gain + t * keep + wz * embed_z(tz, shape)

    def add_sides(u_ref, t_ref, wx_ref, wy_ref, gx, gy):
        for i, at in enumerate((0, nx - 1)):
            u_ref[at] = u_ref[at] + wx_ref[i] * (gx[i] - t_ref[at])
        for i, at in enumerate((0, ny - 1)):
            u_ref[:, at, :] = u_ref[:, at, :] + wy_ref[i] * (gy[i] - t_ref[:, at, :])

    def heat(get_sides, get_heads, ns, *refs):
        mix_ref, den_ref, w_ref, inner_ref, q1_ref, q2_ref, hv_ref, hot1_ref, hot2_ref, u_ref, t0_ref, c_ref = refs[:12]
        got, rest = refs[12 : 12 + ns], refs[12 + ns :]
        h_ref, f_ref, t_ref, wx_ref, wy_ref, *faces = rest[:-1]
        h = sweep(w_ref, den_ref, mix_ref, inner_ref, get_heads(got))
        h_ref[...] = h
        q = jnp.concatenate([q1_ref[...], q2_ref[...]], axis=0)
        flux = q * jnp.sqrt(1.0 + h * h)
        hi = flux.astype(BF16)
        lo = (flux - hi.astype(F32)).astype(BF16)
        lane = (hv_ref[...] % nz).astype(jnp.int16)
        at = lax.broadcasted_iota(jnp.int16, (nz, tri), 0)
        none = jnp.zeros((), BF16)
        parts = jnp.zeros((rows_n, 2 * nz), F32)
        for b in range(0, nb, 2):
            tops, lows = [], []
            for i in range(b, b + 2):
                mine = at == lane[i : i + 1, :]
                tops.append(jnp.where(mine, hi[i : i + 1, :], none))
                lows.append(jnp.where(mine, lo[i : i + 1, :], none))
            wide = jnp.concatenate([jnp.concatenate(tops, axis=1), jnp.concatenate(lows, axis=1)], axis=0)
            hot_ref, o = (hot1_ref, b) if b < nb // 2 else (hot2_ref, b - nb // 2)
            parts = parts + dot(hot_ref[:, o * tri : (o + 2) * tri], wide, 1, 1)
        f = (parts[:, :nz] + parts[:, nz:]).reshape(shape)
        f_ref[...] = f
        t_ref[...] = u_ref[...] + f
        tx, ty = get_sides(got, 0)
        cx, cy = get_sides(got, 1)
        for i, at in enumerate((0, nx - 1)):
            wx_ref[i] = 0.5 * (c_ref[at] + cx[i])
        for i, at in enumerate((0, ny - 1)):
            wy_ref[i] = 0.5 * (c_ref[:, at, :] + cy[i])
        add_sides(t_ref, t0_ref, wx_ref, wy_ref, tx, ty)
        write_faces(faces, specs1, (t_ref[...],))

    def middle(t_ref, f_ref, c_ref, keep_ref, v_ref):
        t = t_ref[...]
        gain, _ = interior(t, c_ref[...])
        v_ref[...] = f_ref[...] + t * keep_ref[...] + gain

    def last(h_ref, v_ref, t_ref, wx_ref, wy_ref, wz_ref, *rest):
        got, (head_ref, out_ref, o_ref, sems) = rest[:-4], rest[-4:]
        heads = pltpu.make_async_copy(h_ref, head_ref, sems.at[0])
        heads.start()
        faces = read_faces(got, specs1, 0)
        z = wz_ref[...] * embed_z(ghosts_of("gz", faces["gz"], (1, rows_n)), shape)
        gx = ghosts_of("gx", faces["gx"], (ny, nz))
        gy = ghosts_of("gy", faces["gy"], (nx, nz))
        step = nx // 2
        copies = [heads]
        for k in range(2):
            part = slice(k * step, (k + 1) * step)
            o_ref[part] = v_ref[part] + z[part]
            if k == 0:
                o_ref[0] = o_ref[0] + wx_ref[0] * (gx[0] - t_ref[0])
            else:
                o_ref[nx - 1] = o_ref[nx - 1] + wx_ref[1] * (gx[1] - t_ref[nx - 1])
            for i, at in enumerate((0, ny - 1)):
                o_ref[part, at, :] = o_ref[part, at, :] + wy_ref[i, part] * (gy[i][part] - t_ref[part, at, :])
            copies.append(pltpu.make_async_copy(o_ref.at[pl.ds(k * step, step)], out_ref.at[pl.ds(k * step, step)], sems.at[k + 1]))
            copies[-1].start()
        for copy in copies:
            copy.wait()

    send, w, t, c, hv, liq, tf, a = call(
        pre,
        [sds((3 * nb + small, tri)), blk, slab, slab, sds((nb, tri), jnp.int32), blk, blk]
        + [sds(local_facet_coupling.shape, BF16)],
        crossing_partner_number.T,
        crossing_permeability.T,
        diagonal_capacity,
        initial_hydraulic_head,
        well_discharge,
        local_facet_coupling,
        stone_thermal_state,
        matrix_diffusivity,
        host_voxel_number,
        liquid_thermal_state,
        transfer_factor,
        scratch=[pltpu.VMEM((links, nb), jnp.int32), pltpu.VMEM((links, nb), F32)]
        + [pltpu.VMEM((nb, tri), F32)] * 2
        + [pltpu.SemaphoreType.DMA((10 + chunks,))],
        hbm=11,
    )
    if pairs:
        slots = meet({k: send for k in range(n - 1, 0, -1) if not k & low}, send)
    mix, *faces = call(rock, [sds((2, nb, n * nb), BF16)] + [sds(s) for _, _, s in specs2], t, c, send)
    got_z = exchange([faces[i] for i in zs], [specs2[i] for i in zs])
    if pairs:
        y_at, xa_at, xb_at = 1, low, 2 * low
        order = {"gx": (xa_at, xb_at), "gy": (y_at,)}
        rides = [order[specs2[i][0]][specs2[i][1]] for i in xy]
        h, *sends = call(
            both,
            [blk] + [sds((nb + 2 * specs2[i][2][1], tri)) for i in xy],
            w,
            a,
            mix,
            send,
            *[slots[k] for k in range(1, n)],
            *[faces[i] for i in xy],
        )
        ride = dict(zip(rides, sends))
        slots = meet({k: ride.get(k, h) for k in range(n - 1, 0, -1) if not k & low or k == y_at | low}, ride[low])
        den = send[2 * nb : 3 * nb]
        got = [h] + [slots[k] for k in range(1, n)]

        def get_heads(refs):
            return jnp.concatenate([r[:nb, :] for r in refs], axis=0)

        def get_sides(refs, j):
            x_rows, y_rows = slice(nb + j * ny, nb + (j + 1) * ny), slice(nb + j * nx, nb + (j + 1) * nx)
            gx = ghosts_of("gx", [refs[xa_at][x_rows, :], refs[xb_at | low][x_rows, :]], (ny, nz))
            return gx, ghosts_of("gy", [refs[y_at][y_rows, :]], (nx, nz))
    else:
        den = send[2 * nb : 3 * nb]
        h = initial_hydraulic_head

        def sweep_body(w_ref, den_ref, mix_ref, inner_ref, heads_ref, h_ref):
            h_ref[...] = sweep(w_ref, den_ref, mix_ref, inner_ref, heads_ref[...])

        for _ in range(SWEEPS - 1):
            heads = lax.all_gather(h, GROUP, axis=0, tiled=True)
            inner = call(inner_body, blk, a, h)
            h = call(sweep_body, blk, w, den, mix, inner, heads)
        got = [lax.all_gather(h, GROUP, axis=0, tiled=True)]
        got += exchange([faces[i] for i in xy], [specs2[i] for i in xy])

        def get_heads(refs):
            return refs[0][...]

        def get_sides(refs, j):
            sides = read_faces(refs[1:], [specs2[i] for i in xy], j)
            return ghosts_of("gx", sides["gx"], (ny, nz)), ghosts_of("gy", sides["gy"], (nx, nz))

    inner = call(inner_body, blk, a, h)
    half = nb // 2
    parts = [
        call(functools.partial(gather, i * half), (sds((half, tri)), sds((rows_n, half * tri), BF16)), t, hv, liq, tf)
        for i in range(2)
    ]
    (q1, hot1), (q2, hot2) = parts
    u, keep, wz = call(base, (slab, slab, slab), t, c, *got_z)
    h, f, t1, wx, wy, *faces = call(
        functools.partial(heat, get_sides, get_heads, len(got)),
        [blk, slab, slab, sds((2, ny, nz)), sds((2, nx, nz))] + [sds(s) for _, _, s in specs1],
        mix,
        den,
        w,
        inner,
        q1,
        q2,
        hv,
        hot1,
        hot2,
        u,
        t,
        c,
        *got,
        scratch=[pltpu.VMEM((2 * nz, nb * tri), BF16)],
    )
    got = exchange(faces, specs1)
    v = call(middle, slab, t1, f, c, keep)
    h, out = call(
        last,
        (blk, slab),
        h,
        v,
        t1,
        wx,
        wy,
        wz,
        *got,
        scratch=[pltpu.VMEM(shape, F32), pltpu.SemaphoreType.DMA((3,))],
        hbm_out=True,
    )
    return (h, out)


def solution(mesh):
    block = P(AXES, None)
    rock = P(*AXES)
    in_specs = (block, block, P(AXES, None, None)) + (block,) * 6 + (rock, rock)

    return jax.shard_map(shards, mesh=mesh, in_specs=in_specs, out_specs=(block, rock), check_vma=False)
```
